32 devices in a mesh: outer: 8 (over z, x), inner: 4 (over y, core).
Axes of the slice: x: 2, y: 2, z: 4, core: 2. Of those that a mesh axis runs over, the one named last changes fastest.
Arguments:
- state_vector: float32 [2, 8, 4, 32768], P(None, 'outer', 'inner'), may hold values from -6 to 6
- gate_matrices: float32 [4, 2, 128, 128], replicated, may hold values from -4 to 4, as said below
Outputs:
- final_state: float32 [2, 8, 4, 32768], P(None, 'outer', 'inner')
- state_rms: float32 [], replicated
The draws below stay inside these ranges and needn't reach their ends.
Inputs may be any that keep to these rules, and one draw needn't show every extreme that they name: `gate_matrices`: each gate is a general complex matrix, not necessarily unitary.
All inputs are finite; a program needn't handle non-finite values.
Results may differ from the reference program's by a relative error of at most 0.000098.
Values sent between devices are 32-bit elements; how exact they have to be, the bound alone decides.
A program may use at most 64 MiB of HBM per device.

```python
import math
import jax
import jax.numpy as jnp
from jax import lax

GATE_QUBITS = 7
AMP_DEV = 32768
N_OUTER = 8
N_INNER = 4


def draw_gate_matrices(key, part):
    size_dim = 2 ** GATE_QUBITS
    key_real, key_imag, key_rough, key_phase = jax.random.split(key, 4)
    noise_real = jnp.clip(jax.random.normal(key_real, (4, size_dim, size_dim), jnp.float32), -3.5, 3.5)
    noise_imag = jnp.clip(jax.random.normal(key_imag, (4, size_dim, size_dim), jnp.float32), -3.5, 3.5)
    qubit_position = jnp.arange(size_dim, dtype=jnp.float32) / (size_dim - 1)
    rising = 3.0 ** qubit_position / 1.82
    roughness = jax.random.uniform(key_rough, (4, size_dim, 1), jnp.float32, 0.8, 1.25)
    row_scale = rising[None, :, None] * roughness
    phase_angle = jax.random.uniform(key_phase, (4, size_dim), jnp.float32, -math.pi, math.pi)
    eye_mat = jnp.eye(size_dim, dtype=jnp.float32)
    stride_spread = 0.4 / math.sqrt(size_dim)
    real_part = row_scale * (eye_mat[None] * jnp.cos(phase_angle)[:, None, :] + stride_spread * noise_real)
    imag_part = row_scale * (eye_mat[None] * jnp.sin(phase_angle)[:, None, :] + stride_spread * noise_imag)
    return jnp.stack([real_part, imag_part], axis=1).astype(jnp.float32)


def shard_levels(key, extent, pieces, least, top_value):
    factor_of = 1.0
    for axis_at, blocks in pieces:
        heights = jax.random.uniform(jax.random.fold_in(jax.random.fold_in(key, 6), axis_at), (blocks,), jnp.float32, least / len(pieces), top_value / len(pieces))
        factor_of = factor_of * jnp.repeat(jnp.exp(heights), extent[axis_at] // blocks).reshape((-1,) + (1,) * (len(extent) - 1 - axis_at))
    return factor_of


def noise(rng, dims, width, limit, cuts=(), held_as=jnp.bfloat16):
    array = jax.random.normal(rng, dims, jnp.float32) * width
    if len(cuts) > 0:
        array = shard_levels(rng, dims, cuts, -0.22, 0.18) * array
    return jnp.clip(array, min=-limit, max=limit).astype(held_as)


def setup_inputs(seed: int = 0) -> dict:
    key_list = jax.random.split(jax.random.key(seed), 3)
    state_vector = noise(key_list[0], (2, N_OUTER, N_INNER, AMP_DEV), 1.0, 6.0, ((1, 8), (2, 4)), jnp.float32)
    gate_matrices = draw_gate_matrices(jax.random.fold_in(key_list[2], 71), 0)
    return {"state_vector": state_vector, "gate_matrices": gate_matrices}


def rows_apply(matrix_pair, blocks):

    def product(gate_matrix, value_entries):
        return jnp.einsum('ng,wgy->wny', gate_matrix, value_entries, precision=lax.Precision.HIGHEST)
    real_out = product(matrix_pair[0], blocks[0]) - product(matrix_pair[1], blocks[1])
    imag_out = product(matrix_pair[0], blocks[1]) + product(matrix_pair[1], blocks[0])
    return jnp.stack([real_out, imag_out])

def low_apply(matrix_pair, blocks):

    def product(gate_matrix, value_entries):
        return jnp.einsum('km,xm->xk', gate_matrix, value_entries, precision=lax.Precision.HIGHEST)
    real_out = product(matrix_pair[0], blocks[0]) - product(matrix_pair[1], blocks[1])
    imag_out = product(matrix_pair[0], blocks[1]) + product(matrix_pair[1], blocks[0])
    return jnp.stack([real_out, imag_out])

def reference(state_vector, gate_matrices):
    outer_count = state_vector.shape[1]
    inner_count = state_vector.shape[2]
    amp_count = state_vector.shape[3]
    gate_dim = gate_matrices.shape[2]
    width_low = amp_count // gate_dim
    amplitude_values = rows_apply(gate_matrices[0], state_vector.reshape(2, -1, gate_dim, gate_dim))
    outer_rest = gate_dim // outer_count
    amplitude_values = amplitude_values.reshape(2, outer_count, inner_count, outer_count, outer_rest, width_low)
    amplitude_values = amplitude_values.transpose(0, 2, 3, 1, 4, 5).reshape(2, inner_count * outer_count, gate_dim, width_low)
    amplitude_values = rows_apply(gate_matrices[1], amplitude_values)
    amplitude_values = amplitude_values.reshape(2, inner_count, outer_count, outer_count, outer_rest, width_low)
    amplitude_values = amplitude_values.transpose(0, 3, 1, 2, 4, 5)
    inner_rest = gate_dim // inner_count
    amplitude_values = amplitude_values.reshape(2, outer_count, inner_count, inner_count, inner_rest, width_low)
    amplitude_values = amplitude_values.transpose(0, 1, 3, 2, 4, 5).reshape(2, outer_count * inner_count, gate_dim, width_low)
    amplitude_values = rows_apply(gate_matrices[2], amplitude_values)
    amplitude_values = amplitude_values.reshape(2, outer_count, inner_count, inner_count, inner_rest, width_low)
    amplitude_values = amplitude_values.transpose(0, 1, 3, 2, 4, 5)
    amplitude_values = low_apply(gate_matrices[3], amplitude_values.reshape(2, -1, gate_dim))
    amplitude_values = amplitude_values.reshape(2, outer_count, inner_count, amp_count)
    total_sum = jnp.sum(amplitude_values * amplitude_values)
    amplitude_total = outer_count * inner_count * amp_count
    root_mean = jnp.sqrt(total_sum / amplitude_total)
    final_state = amplitude_values / root_mean
    return (final_state, root_mean)
```

```python
import functools

import jax
import jax.numpy as jnp
from jax import lax
from jax.experimental import pallas as pl
from jax.experimental.pallas import tpu as pltpu
from jax.sharding import PartitionSpec as P

MESH = pl.DeviceIdType.MESH
TRADE_LIMIT = 56_150_000
LIMIT = 16 * 1024 * 1024


def halves(values):
    high = values.astype(jnp.bfloat16)
    low = (values - high.astype(jnp.float32)).astype(jnp.bfloat16)
    return high, low


def product(left, right, dims):
    def one(a, b):
        return lax.dot_general(a, b, (dims, ((), ())), preferred_element_type=jnp.float32)

    return one(left[0], right[0]) + (one(left[0], right[1]) + one(left[1], right[0]))


def complex_matrix(real, imag):
    top = jnp.concatenate([real, -imag], axis=1)
    bottom = jnp.concatenate([imag, real], axis=1)
    return halves(jnp.concatenate([top, bottom], axis=0))


def spread(position, count):
    half, rest = count // 2, position // 2
    return (position % 2) * half + (rest % 2) * (half // 2) + rest // 2


def kernel(
    n_outer, n_inner, chunks, state_in, gates_in, held_c, sums,
    state, gates, sent_a, held_a, sent_b, held_b, sent_c, part, fetched,
    send_a, recv_a, send_b, recv_b, send_c, recv_c, send_s, recv_s,
):
    def fetch(at):
        if at == 0:
            return pltpu.make_async_copy(state_in, state, fetched.at[0])
        return pltpu.make_async_copy(gates_in.at[at - 1], gates.at[at - 1], fetched.at[at])

    for at in (0, 1, 4, 2, 3):
        fetch(at).start()
    dim = gates.shape[2]
    passive = state.shape[1] // dim
    sub = passive // chunks
    step = dim // chunks
    rows_outer = dim // n_outer * sub
    rows_inner = dim // n_inner * sub
    ratio = n_outer // n_inner
    n_all = n_outer * n_inner
    outer, inner = lax.axis_index("outer"), lax.axis_index("inner")
    me = outer * n_inner + inner

    def block(ref, chunk, at, rows):
        return ref.at[chunk, :, pl.ds(pl.multiple_of(at * rows, rows), rows), :]

    def remote(src, dst, send, recv, target):
        return pltpu.make_async_remote_copy(
            src_ref=src, dst_ref=dst, send_sem=send, recv_sem=recv,
            device_id=target, device_id_type=MESH,
        )

    far_first = sorted(range(n_outer), key=lambda k: abs(2 * k - n_outer))

    def everyone(act):
        if n_all > 64:

            def body(k, carry):
                one(act, k // n_inner, k % n_inner)
                return carry

            lax.fori_loop(1, n_all, body, 0)
            return
        for a in far_first:
            for b in range(n_inner):
                if a or b:
                    one(act, a, b)

    def one(act, a, b):
        ahead = ((outer + a) % n_outer, (inner + b) % n_inner)
        behind = ((outer + n_outer - a) % n_outer, (inner + n_inner - b) % n_inner)
        act(a * n_inner + b, ahead, behind)

    barrier = pltpu.get_barrier_semaphore()

    for k in range(1, n_outer):
        pl.semaphore_signal(
            barrier, inc=1, device_id=((outer + k) % n_outer, inner), device_id_type=MESH
        )
    for k in range(1, n_inner):
        pl.semaphore_signal(
            barrier, inc=1, device_id=(outer, (inner + k) % n_inner), device_id_type=MESH
        )

    def load(ref, chunk):
        return jnp.concatenate(
            [
                jnp.concatenate(
                    [ref[chunk, c, pl.ds(b, dim, stride=sub), :] for b in range(sub)], axis=1
                )
                for c in range(2)
            ],
            axis=0,
        )

    def store(ref, chunk, values):
        for c in range(2):
            for b in range(sub):
                ref[chunk, c, pl.ds(b, dim, stride=sub), :] = values[
                    c * dim : (c + 1) * dim, b * dim : (b + 1) * dim
                ]

    def low_gate(values):
        rows = values.shape[0] // 2
        matrix = complex_matrix(gates[3, 0], gates[3, 1])
        columns = []
        for b in range(values.shape[1] // dim):
            both = values[:, b * dim : (b + 1) * dim]
            wide = jnp.concatenate([both[:rows], both[rows:]], axis=1)
            wide = product(halves(wide), matrix, ((1,), (1,)))
            columns.append(jnp.concatenate([wide[:, :dim], wide[:, dim:]], axis=0))
        return jnp.concatenate(columns, axis=1)

    fetch(0).wait()
    fetch(1).wait()
    first = halves(
        jnp.concatenate(
            [
                jnp.concatenate(
                    [state[c, w * dim : (w + 1) * dim, :] for w in range(passive)], axis=1
                )
                for c in range(2)
            ],
            axis=0,
        )
    )

    def trade_a(chunk):
        for k in far_first[:-1]:
            to = (outer + k) % n_outer
            remote(
                block(sent_a, chunk, spread(to, n_outer), rows_outer),
                block(held_a, chunk, outer, rows_outer),
                send_a.at[chunk, to], recv_a.at[chunk, outer], (to, inner),
            ).start()
        pltpu.make_async_copy(
            block(sent_a, chunk, spread(outer, n_outer), rows_outer),
            block(held_a, chunk, outer, rows_outer),
            recv_a.at[chunk, outer],
        ).start()

    for chunk in range(chunks):
        pick = pl.ds(chunk, step, stride=chunks)
        matrix = complex_matrix(gates[0, 0, pick, :], gates[0, 1, pick, :])
        values = product(matrix, first, ((1,), (0,)))
        if chunk > 0:
            if chunk == 1:
                fetch(4).wait()
            values = low_gate(values)
        for c in range(2):
            for w in range(passive):
                sent_a[chunk, c, w * step : (w + 1) * step, :] = values[
                    c * step : (c + 1) * step, w * dim : (w + 1) * dim
                ]
        if chunk == 0:
            pl.semaphore_wait(barrier, n_outer + n_inner - 2)
        trade_a(chunk)

    fetch(2).wait()
    matrix = complex_matrix(gates[1, 0], gates[1, 1])
    mine = spread(outer, n_outer)
    column, within = mine // ratio, mine % ratio
    slot = inner * ratio + within
    for chunk in range(chunks):
        for k in range(n_outer):
            spot = block(held_a, chunk, k, rows_outer)
            remote(spot, spot, send_a.at[chunk, k], recv_a.at[chunk, k], (outer, inner)).wait_recv()
        values = halves(load(held_a, chunk))
        store(sent_b, chunk, product(matrix, values, ((1,), (0,))))
        for k in far_first:
            to = (outer + k) % n_outer
            src = block(sent_b, chunk, to, rows_outer)
            dst = block(held_b, chunk, slot, rows_outer)
            copy = remote(
                src, dst, send_b.at[chunk, to], recv_b.at[chunk, slot], (to, column)
            )
            if k > 0:
                copy.start()
            else:
                pl.when(column != inner)(copy.start)
                pl.when(column == inner)(
                    pltpu.make_async_copy(src, dst, recv_b.at[chunk, slot]).start
                )

    fetch(3).wait()
    matrix = complex_matrix(gates[2, 0], gates[2, 1])
    total = jnp.zeros((1, dim), jnp.float32)
    own = pltpu.make_async_copy(part, sums.at[me], recv_s.at[0])

    def share(k, ahead, behind):
        remote(part, sums.at[me], send_s.at[k], recv_s.at[k], ahead).start()

    for chunk in range(chunks):
        for k in range(n_outer):
            spot = block(held_b, chunk, k, rows_outer)
            remote(spot, spot, send_b.at[chunk, k], recv_b.at[chunk, k], (outer, inner)).wait_recv()
        values = product(matrix, halves(load(held_b, chunk)), ((1,), (0,)))
        if chunk == 0:
            if chunks == 1:
                fetch(4).wait()
            values = low_gate(values)
        for b in range(sub):
            piece = values[:, b * dim : (b + 1) * dim]
            total = total + jnp.sum(piece * piece, axis=0, keepdims=True)
        if chunk == chunks - 1:
            part[...] = total
            everyone(share)
            own.start()
        store(sent_c, chunk, values)
        for k in range(1, n_inner):
            to = (inner + k) % n_inner
            remote(
                block(sent_c, chunk, to, rows_inner),
                block(held_c, chunk, inner, rows_inner),
                send_c.at[chunk, to], recv_c.at[chunk, inner], (outer, to),
            ).start()
        pltpu.make_async_copy(
            block(sent_c, chunk, inner, rows_inner),
            block(held_c, chunk, inner, rows_inner),
            recv_c.at[chunk, inner],
        ).start()

    def arrived(k, ahead, behind):
        spot = sums.at[behind[0] * n_inner + behind[1]]
        remote(part, spot, send_s.at[k], recv_s.at[k], ahead).wait_recv()

    def left(k, ahead, behind):
        remote(part, sums.at[me], send_s.at[k], recv_s.at[k], ahead).wait_send()

    for chunk in range(chunks):
        for k in range(n_inner):
            spot = block(held_c, chunk, k, rows_inner)
            remote(spot, spot, send_c.at[chunk, k], recv_c.at[chunk, k], (outer, inner)).wait_recv()

    for chunk in range(chunks):
        for k in range(1, n_outer):
            to = (outer + k) % n_outer
            spot = block(sent_a, chunk, to, rows_outer)
            remote(spot, spot, send_a.at[chunk, to], recv_a.at[chunk, to], (to, inner)).wait_send()
        for k in range(n_outer):
            to = (outer + k) % n_outer
            spot = block(sent_b, chunk, to, rows_outer)
            copy = remote(spot, spot, send_b.at[chunk, to], recv_b.at[chunk, to], (to, column))
            if k > 0:
                copy.wait_send()
            else:
                pl.when(column != inner)(copy.wait_send)
        for k in range(1, n_inner):
            to = (inner + k) % n_inner
            spot = block(sent_c, chunk, to, rows_inner)
            remote(spot, spot, send_c.at[chunk, to], recv_c.at[chunk, to], (outer, to)).wait_send()
    everyone(left)
    own.wait()
    everyone(arrived)


def finish(n_all, values, sums, out, rms):
    chunks, _, rows, dim = values.shape
    whole = jnp.sum(jnp.sum(sums[...], axis=0), axis=1, keepdims=True)
    root = jnp.sqrt(whole / (n_all * chunks * rows * dim))
    rms[...] = root
    scale = jnp.broadcast_to(1.0 / root, (8, dim))
    for chunk in range(chunks):
        for c in range(2):
            scaled = values[chunk, c].reshape(-1, 8, dim) * scale[None]
            out[c, pl.ds(chunk, rows, stride=chunks), :] = scaled.reshape(-1, dim)


def shards(n_outer, n_inner, state_vector, gate_matrices):
    dim = gate_matrices.shape[2]
    amp_count = state_vector.shape[3]
    rows = amp_count // dim
    passive = rows // dim
    chunks = passive if (dim // n_outer) % 8 == 0 else 1
    held = pltpu.VMEM((chunks, 2, rows // chunks, dim), jnp.float32)
    n_all = n_outer * n_inner
    dma = pltpu.SemaphoreType.DMA
    vmem = pl.BlockSpec(memory_space=pltpu.VMEM)
    hbm = pl.BlockSpec(memory_space=pltpu.HBM)
    anywhere = pl.BlockSpec(memory_space=pl.ANY)
    values, sums = pl.pallas_call(
        functools.partial(kernel, n_outer, n_inner, chunks),
        out_shape=(
            jax.ShapeDtypeStruct((chunks, 2, rows // chunks, dim), jnp.float32),
            jax.ShapeDtypeStruct((n_all, 1, dim), jnp.float32),
        ),
        in_specs=[hbm, hbm],
        out_specs=(anywhere, anywhere),
        scratch_shapes=[
            pltpu.VMEM((2, rows, dim), jnp.float32),
            pltpu.VMEM(gate_matrices.shape, jnp.float32),
        ]
        + [held] * 5
        + [pltpu.VMEM((1, dim), jnp.float32), dma((5,))]
        + [dma((chunks, n_outer))] * 4
        + [dma((chunks, n_inner))] * 2
        + [dma((n_all,))] * 2,
        compiler_params=pltpu.CompilerParams(
            collective_id=0, has_side_effects=True, vmem_limit_bytes=TRADE_LIMIT
        ),
    )(state_vector.reshape(2, rows, dim), gate_matrices)
    final_state, root = pl.pallas_call(
        functools.partial(finish, n_all),
        out_shape=(
            jax.ShapeDtypeStruct((2, rows, dim), jnp.float32),
            jax.ShapeDtypeStruct((1, 1), jnp.float32),
        ),
        in_specs=[vmem, vmem],
        out_specs=(vmem, vmem),
        compiler_params=pltpu.CompilerParams(vmem_limit_bytes=LIMIT),
    )(values, sums)
    return final_state.reshape(state_vector.shape), root.reshape(())


def relabel(tiles, names, order):
    count = len(names)
    places = [count - 1 - names.index(name) for name in order]
    picked = []
    for at in range(len(tiles)):
        bits = [(at >> (count - 1 - j)) & 1 for j in range(count)]
        picked.append(tiles[sum(bit << place for bit, place in zip(bits, places))])
    return picked


def swap(tiles, names, major, lane):
    step = 1 << (len(names) - 1 - names.index(major))
    lows = [at for at in range(len(tiles)) if not at & step]
    low = jnp.concatenate([tiles[at] for at in lows], axis=0)
    high = jnp.concatenate([tiles[at + step] for at in lows], axis=0)
    size = low.shape[1]
    first = lax.broadcasted_iota(jnp.int32, low.shape, 1) // lane % 2 == 0
    new_low = jnp.where(first, low, pltpu.roll(high, lane, 1))
    new_high = jnp.where(first, pltpu.roll(low, size - lane, 1), high)
    out = list(tiles)
    for j, at in enumerate(lows):
        out[at] = new_low[j * 8 : (j + 1) * 8]
        out[at + step] = new_high[j * 8 : (j + 1) * 8]
    return out


def split(values):
    return [values[at * 8 : (at + 1) * 8] for at in range(values.shape[0] // 8)]


def join(tiles):
    return jnp.concatenate(tiles, axis=0)


def rename(names, old, new):
    return [new if name == old else name for name in names]


def bits(name, count):
    return [name + str(j) for j in reversed(range(count))]


def fast_kernel(
    n_outer, n_inner, state_in, gates_in, held_b, sums,
    state, gates, sent_a, held_a, sent_b, part, fetched,
    send_a, recv_a, send_b, recv_b, send_s, recv_s, own_s,
):
    def fetch(at):
        if at == 0:
            return pltpu.make_async_copy(state_in, state, fetched.at[0])
        return pltpu.make_async_copy(gates_in.at[at - 1], gates.at[at - 1], fetched.at[at])

    for at in (0, 1, 4, 2, 3):
        fetch(at).start()
    dim = gates.shape[2]
    chunks = state.shape[1] // dim
    n_all = n_outer * n_inner
    n_bits, o_bits, i_bits = (v.bit_length() - 1 for v in (n_all, n_outer, n_inner))
    outer, inner = lax.axis_index("outer"), lax.axis_index("inner")
    me = outer * n_inner + inner

    def peer(k):
        a, b = outer, inner
        for j in range(o_bits):
            if (k // n_inner) >> j & 1:
                a = a + (1 - 2 * (outer // 2**j % 2)) * 2**j
        for j in range(i_bits):
            if (k % n_inner) >> j & 1:
                b = b + (1 - 2 * (inner // 2**j % 2)) * 2**j
        return a, b

    half = n_all // 2
    order = []
    for k in reversed(range(half)):
        order += [k + half] + ([k] if k else [])
    barrier = pltpu.get_barrier_semaphore()
    for k in order:
        pl.semaphore_signal(barrier, inc=1, device_id=peer(k), device_id_type=MESH)

    def remote(src, dst, send, recv, target):
        return pltpu.make_async_remote_copy(
            src_ref=src, dst_ref=dst, send_sem=send, recv_sem=recv,
            device_id=target, device_id_type=MESH,
        )

    def tile(ref, chunk, at):
        return ref.at[chunk, pl.ds(pl.multiple_of(at * 8, 8), 8), :]

    def trade(sent, held, send, recv, chunk):
        for k in order:
            a, b = peer(k)
            remote(
                tile(sent, chunk, a * n_inner + b), tile(held, chunk, me),
                send.at[chunk], recv.at[chunk], (a, b),
            ).start()
        pltpu.make_async_copy(
            tile(sent, chunk, me), tile(held, chunk, me), recv.at[chunk]
        ).start()

    def arrived(held, send, recv, chunk):
        spot = held.at[chunk]
        remote(spot, spot, send.at[chunk], recv.at[chunk], (outer, inner)).wait_recv()

    def left(sent, send, recv, chunk):
        spot = sent.at[chunk, pl.ds(0, (n_all - 1) * 8), :]
        remote(spot, spot, send.at[chunk], recv.at[chunk], (outer, inner)).wait_send()

    top = dim // 2
    fetch(1).wait()

    def rows0(c):
        return jnp.concatenate(
            [
                gates[0, c, pl.ds(high * top + low, top // 2, stride=2), :]
                for high in range(2)
                for low in range(2)
            ],
            axis=0,
        )

    first = complex_matrix(rows0(0), rows0(1))
    fetch(4).wait()
    real, imag = gates[3, 0], gates[3, 1]
    low = []
    for high in range(2):
        spot = slice(high * top, (high + 1) * top)
        low.append(jnp.concatenate([real[spot], -imag[spot]], axis=1))
        low.append(jnp.concatenate([imag[spot], real[spot]], axis=1))
    low = halves(jnp.concatenate(low, axis=0))
    fetch(0).wait()
    for chunk in range(chunks):
        values = jnp.concatenate(
            [state[c, chunk * dim : (chunk + 1) * dim, :] for c in range(2)], axis=0
        )
        values = product(first, halves(values), ((1,), (0,)))
        wide = jnp.concatenate([values[:dim], values[dim:]], axis=1)
        wide = product(halves(wide), low, ((1,), (1,)))
        tiles = split(jnp.concatenate([wide[:, :dim], wide[:, dim:]], axis=0))
        names = ["b6", "b13", "b7", "b12", "b11"]
        tiles = swap(tiles, names, "b12", dim // 4)
        names = rename(names, "b12", "b5")
        tiles = swap(tiles, names, "b11", dim // 8)
        sent_a[chunk] = join(tiles)
        if chunk == 0:
            pl.semaphore_wait(barrier, n_all - 1)
        trade(sent_a, held_a, send_a, recv_a, chunk)

    fetch(2).wait()
    second = complex_matrix(gates[1, 0], gates[1, 1])
    fetch(3).wait()
    third = complex_matrix(gates[2, 0], gates[2, 1])
    o_names, i_names = bits("o", o_bits), bits("i", i_bits)
    total = jnp.zeros((1, dim), jnp.float32)
    for chunk in range(chunks):
        arrived(held_a, send_a, recv_a, chunk)
        tiles = split(held_a[chunk])
        names = o_names + i_names
        tiles = swap(tiles, names, "i1", dim // 2)
        names = rename(names, "i1", "c")
        tiles = swap(tiles, names, "i0", dim // 8)
        names = rename(names, "i0", "b11")
        rows = ["c"] + o_names + ["b11"]
        values = product(second, halves(join(relabel(tiles, names, rows))), ((1,), (0,)))
        tiles, names = split(values), rows
        for name, new, lane in (("o2", "i1", 2), ("o1", "b12", 4), ("o0", "i0", 8)):
            tiles = swap(tiles, names, name, dim // lane)
            names = rename(names, name, new)
        rows = ["c"] + i_names + ["b12", "b11"]
        values = product(third, halves(join(relabel(tiles, names, rows))), ((1,), (0,)))
        total = total + jnp.sum(values * values, axis=0, keepdims=True)
        if chunk == chunks - 1:
            part[...] = total
            for k in order:
                remote(part, sums.at[me], send_s, recv_s, peer(k)).start()
            pltpu.make_async_copy(part, sums.at[me], own_s).start()
        tiles, names = split(values), rows
        for name, new, lane in (("c", "o2", 2), ("b12", "o1", 4), ("b11", "o0", 8)):
            tiles = swap(tiles, names, name, dim // lane)
            names = rename(names, name, new)
        sent_b[chunk] = join(relabel(tiles, names, o_names + i_names))
        trade(sent_b, held_b, send_b, recv_b, chunk)

    for chunk in range(chunks):
        left(sent_a, send_a, recv_a, chunk)
    everyone = sums.at[pl.ds(0, n_all - 1)]
    remote(everyone, everyone, send_s, recv_s, (outer, inner)).wait()
    pltpu.make_async_copy(part, sums.at[me], own_s).wait()
    for chunk in range(chunks):
        arrived(held_b, send_b, recv_b, chunk)
        left(sent_b, send_b, recv_b, chunk)


def fast_finish(n_all, values, sums, out, rms):
    chunks, rows, dim = values.shape
    half = rows // 2
    whole = jnp.sum(jnp.sum(sums[...], axis=0), axis=1, keepdims=True)
    root = jnp.sqrt(whole / (n_all * chunks * half * dim))
    rms[...] = root
    scale = jnp.broadcast_to(1.0 / root, (8, dim))
    for chunk in range(chunks):
        tiles = split(values[chunk])
        names = ["b6", "b13", "b7", "b5", "b4"]
        for name, new, lane in (("b6", "c", 2), ("b5", "b12", 4), ("b4", "b11", 8)):
            tiles = swap(tiles, names, name, dim // lane)
            names = rename(names, name, new)
        tiles = relabel(tiles, names, ["c", "b13", "b12", "b11", "b7"])
        for at in range(len(tiles)):
            c, rest = divmod(at, len(tiles) // 2)
            start = chunk * half + rest // 2 * 16 + rest % 2
            out[c, pl.ds(start, 8, stride=2), :] = tiles[at] * scale


def fast_shards(n_outer, n_inner, state_vector, gate_matrices):
    dim = gate_matrices.shape[2]
    rows = state_vector.shape[3] // dim
    chunks = rows // dim
    n_all = n_outer * n_inner
    held = pltpu.VMEM((chunks, n_all * 8, dim), jnp.float32)
    dma = pltpu.SemaphoreType.DMA
    vmem = pl.BlockSpec(memory_space=pltpu.VMEM)
    hbm = pl.BlockSpec(memory_space=pltpu.HBM)
    anywhere = pl.BlockSpec(memory_space=pl.ANY)
    values, sums = pl.pallas_call(
        functools.partial(fast_kernel, n_outer, n_inner),
        out_shape=(
            jax.ShapeDtypeStruct((chunks, n_all * 8, dim), jnp.float32),
            jax.ShapeDtypeStruct((n_all, 1, dim), jnp.float32),
        ),
        in_specs=[hbm, hbm],
        out_specs=(anywhere, anywhere),
        scratch_shapes=[
            pltpu.VMEM((2, rows, dim), jnp.float32),
            pltpu.VMEM(gate_matrices.shape, jnp.float32),
        ]
        + [held] * 3
        + [pltpu.VMEM((1, dim), jnp.float32), dma((5,))]
        + [dma((chunks,))] * 4
        + [dma(())] * 3,
        compiler_params=pltpu.CompilerParams(
            collective_id=0, has_side_effects=True, vmem_limit_bytes=TRADE_LIMIT
        ),
    )(state_vector.reshape(2, rows, dim), gate_matrices)
    final_state, root = pl.pallas_call(
        functools.partial(fast_finish, n_all),
        out_shape=(
            jax.ShapeDtypeStruct((2, rows, dim), jnp.float32),
            jax.ShapeDtypeStruct((1, 1), jnp.float32),
        ),
        in_specs=[vmem, vmem],
        out_specs=(vmem, vmem),
        compiler_params=pltpu.CompilerParams(vmem_limit_bytes=LIMIT),
    )(values, sums)
    return final_state.reshape(state_vector.shape), root.reshape(())


def fits(n_outer, n_inner, state_vector, gate_matrices):
    dim = gate_matrices.shape[2]
    rows = state_vector.shape[3] // dim
    return (
        rows == 2 * dim
        and n_outer * n_inner * 8 == 2 * dim
        and dim == n_outer * 16
        and dim == n_inner * 32
    )


def shards_of(n_outer, n_inner, state_vector, gate_matrices):
    run = fast_shards if fits(n_outer, n_inner, state_vector, gate_matrices) else shards
    return run(n_outer, n_inner, state_vector, gate_matrices)


def solution(mesh):
    in_specs = (P(None, "outer", "inner", None), P())
    out_specs = (P(None, "outer", "inner", None), P())
    body = functools.partial(shards_of, mesh.shape["outer"], mesh.shape["inner"])
    return jax.shard_map(body, mesh=mesh, in_specs=in_specs, out_specs=out_specs, check_vma=False)
```

```python
import functools

import jax
import jax.numpy as jnp
from jax import lax
from jax.experimental import pallas as pl
from jax.experimental.pallas import tpu as pltpu
from jax.sharding import PartitionSpec as P

MESH = pl.DeviceIdType.MESH
TRADE_LIMIT = 56_150_000
LIMIT = 16 * 1024 * 1024


def halves(values):
    high = values.astype(jnp.bfloat16)
    low = (values - high.astype(jnp.float32)).astype(jnp.bfloat16)
    return high, low


def product(left, right, dims):
    def one(a, b):
        return lax.dot_general(a, b, (dims, ((), ())), preferred_element_type=jnp.float32)

    return one(left[0], right[0]) + (one(left[0], right[1]) + one(left[1], right[0]))


def complex_matrix(real, imag):
    top = jnp.concatenate([real, -imag], axis=1)
    bottom = jnp.concatenate([imag, real], axis=1)
    return halves(jnp.concatenate([top, bottom], axis=0))


def spread(position, count):
    half, rest = count // 2, position // 2
    return (position % 2) * half + (rest % 2) * (half // 2) + rest // 2


def kernel(
    n_outer, n_inner, chunks, state_in, gates_in, held_c, sums,
    state, gates, sent_a, held_a, sent_b, held_b, sent_c, part, fetched,
    send_a, recv_a, send_b, recv_b, send_c, recv_c, send_s, recv_s,
):
    def fetch(at):
        if at == 0:
            return pltpu.make_async_copy(state_in, state, fetched.at[0])
        return pltpu.make_async_copy(gates_in.at[at - 1], gates.at[at - 1], fetched.at[at])

    for at in (0, 1, 4, 2, 3):
        fetch(at).start()
    dim = gates.shape[2]
    passive = state.shape[1] // dim
    sub = passive // chunks
    step = dim // chunks
    rows_outer = dim // n_outer * sub
    rows_inner = dim // n_inner * sub
    ratio = n_outer // n_inner
    n_all = n_outer * n_inner
    outer, inner = lax.axis_index("outer"), lax.axis_index("inner")
    me = outer * n_inner + inner

    def block(ref, chunk, at, rows):
        return ref.at[chunk, :, pl.ds(pl.multiple_of(at * rows, rows), rows), :]

    def remote(src, dst, send, recv, target):
        return pltpu.make_async_remote_copy(
            src_ref=src, dst_ref=dst, send_sem=send, recv_sem=recv,
            device_id=target, device_id_type=MESH,
        )

    far_first = sorted(range(n_outer), key=lambda k: abs(2 * k - n_outer))

    def everyone(act):
        if n_all > 64:

            def body(k, carry):
                one(act, k // n_inner, k % n_inner)
                return carry

            lax.fori_loop(1, n_all, body, 0)
            return
        for a in far_first:
            for b in range(n_inner):
                if a or b:
                    one(act, a, b)

    def one(act, a, b):
        ahead = ((outer + a) % n_outer, (inner + b) % n_inner)
        behind = ((outer + n_outer - a) % n_outer, (inner + n_inner - b) % n_inner)
        act(a * n_inner + b, ahead, behind)

    barrier = pltpu.get_barrier_semaphore()

    for k in range(1, n_outer):
        pl.semaphore_signal(
            barrier, inc=1, device_id=((outer + k) % n_outer, inner), device_id_type=MESH
        )
    for k in range(1, n_inner):
        pl.semaphore_signal(
            barrier, inc=1, device_id=(outer, (inner + k) % n_inner), device_id_type=MESH
        )

    def load(ref, chunk):
        return jnp.concatenate(
            [
                jnp.concatenate(
                    [ref[chunk, c, pl.ds(b, dim, stride=sub), :] for b in range(sub)], axis=1
                )
                for c in range(2)
            ],
            axis=0,
        )

    def store(ref, chunk, values):
        for c in range(2):
            for b in range(sub):
                ref[chunk, c, pl.ds(b, dim, stride=sub), :] = values[
                    c * dim : (c + 1) * dim, b * dim : (b + 1) * dim
                ]

    def low_gate(values):
        rows = values.shape[0] // 2
        matrix = complex_matrix(gates[3, 0], gates[3, 1])
        columns = []
        for b in range(values.shape[1] // dim):
            both = values[:, b * dim : (b + 1) * dim]
            wide = jnp.concatenate([both[:rows], both[rows:]], axis=1)
            wide = product(halves(wide), matrix, ((1,), (1,)))
            columns.append(jnp.concatenate([wide[:, :dim], wide[:, dim:]], axis=0))
        return jnp.concatenate(columns, axis=1)

    fetch(0).wait()
    fetch(1).wait()
    first = halves(
        jnp.concatenate(
            [
                jnp.concatenate(
                    [state[c, w * dim : (w + 1) * dim, :] for w in range(passive)], axis=1
                )
                for c in range(2)
            ],
            axis=0,
        )
    )

    def trade_a(chunk):
        for k in far_first[:-1]:
            to = (outer + k) % n_outer
            remote(
                block(sent_a, chunk, spread(to, n_outer), rows_outer),
                block(held_a, chunk, outer, rows_outer),
                send_a.at[chunk, to], recv_a.at[chunk, outer], (to, inner),
            ).start()
        pltpu.make_async_copy(
            block(sent_a, chunk, spread(outer, n_outer), rows_outer),
            block(held_a, chunk, outer, rows_outer),
            recv_a.at[chunk, outer],
        ).start()

    for chunk in range(chunks):
        pick = pl.ds(chunk, step, stride=chunks)
        matrix = complex_matrix(gates[0, 0, pick, :], gates[0, 1, pick, :])
        values = product(matrix, first, ((1,), (0,)))
        if chunk > 0:
            if chunk == 1:
                fetch(4).wait()
            values = low_gate(values)
        for c in range(2):
            for w in range(passive):
                sent_a[chunk, c, w * step : (w + 1) * step, :] = values[
                    c * step : (c + 1) * step, w * dim : (w + 1) * dim
                ]
        if chunk == 0:
            pl.semaphore_wait(barrier, n_outer + n_inner - 2)
        trade_a(chunk)

    fetch(2).wait()
    matrix = complex_matrix(gates[1, 0], gates[1, 1])
    mine = spread(outer, n_outer)
    column, within = mine // ratio, mine % ratio
    slot = inner * ratio + within
    for chunk in range(chunks):
        for k in range(n_outer):
            spot = block(held_a, chunk, k, rows_outer)
            remote(spot, spot, send_a.at[chunk, k], recv_a.at[chunk, k], (outer, inner)).wait_recv()
        values = halves(load(held_a, chunk))
        store(sent_b, chunk, product(matrix, values, ((1,), (0,))))
        for k in far_first:
            to = (outer + k) % n_outer
            src = block(sent_b, chunk, to, rows_outer)
            dst = block(held_b, chunk, slot, rows_outer)
            copy = remote(
                src, dst, send_b.at[chunk, to], recv_b.at[chunk, slot], (to, column)
            )
            if k > 0:
                copy.start()
            else:
                pl.when(column != inner)(copy.start)
                pl.when(column == inner)(
                    pltpu.make_async_copy(src, dst, recv_b.at[chunk, slot]).start
                )

    fetch(3).wait()
    matrix = complex_matrix(gates[2, 0], gates[2, 1])
    total = jnp.zeros((1, dim), jnp.float32)
    own = pltpu.make_async_copy(part, sums.at[me], recv_s.at[0])

    def share(k, ahead, behind):
        remote(part, sums.at[me], send_s.at[k], recv_s.at[k], ahead).start()

    for chunk in range(chunks):
        for k in range(n_outer):
            spot = block(held_b, chunk, k, rows_outer)
            remote(spot, spot, send_b.at[chunk, k], recv_b.at[chunk, k], (outer, inner)).wait_recv()
        values = product(matrix, halves(load(held_b, chunk)), ((1,), (0,)))
        if chunk == 0:
            if chunks == 1:
                fetch(4).wait()
            values = low_gate(values)
        for b in range(sub):
            piece = values[:, b * dim : (b + 1) * dim]
            total = total + jnp.sum(piece * piece, axis=0, keepdims=True)
        if chunk == chunks - 1:
            part[...] = total
            everyone(share)
            own.start()
        store(sent_c, chunk, values)
        for k in range(1, n_inner):
            to = (inner + k) % n_inner
            remote(
                block(sent_c, chunk, to, rows_inner),
                block(held_c, chunk, inner, rows_inner),
                send_c.at[chunk, to], recv_c.at[chunk, inner], (outer, to),
            ).start()
        pltpu.make_async_copy(
            block(sent_c, chunk, inner, rows_inner),
            block(held_c, chunk, inner, rows_inner),
            recv_c.at[chunk, inner],
        ).start()

    def arrived(k, ahead, behind):
        spot = sums.at[behind[0] * n_inner + behind[1]]
        remote(part, spot, send_s.at[k], recv_s.at[k], ahead).wait_recv()

    def left(k, ahead, behind):
        remote(part, sums.at[me], send_s.at[k], recv_s.at[k], ahead).wait_send()

    for chunk in range(chunks):
        for k in range(n_inner):
            spot = block(held_c, chunk, k, rows_inner)
            remote(spot, spot, send_c.at[chunk, k], recv_c.at[chunk, k], (outer, inner)).wait_recv()

    for chunk in range(chunks):
        for k in range(1, n_outer):
            to = (outer + k) % n_outer
            spot = block(sent_a, chunk, to, rows_outer)
            remote(spot, spot, send_a.at[chunk, to], recv_a.at[chunk, to], (to, inner)).wait_send()
        for k in range(n_outer):
            to = (outer + k) % n_outer
            spot = block(sent_b, chunk, to, rows_outer)
            copy = remote(spot, spot, send_b.at[chunk, to], recv_b.at[chunk, to], (to, column))
            if k > 0:
                copy.wait_send()
            else:
                pl.when(column != inner)(copy.wait_send)
        for k in range(1, n_inner):
            to = (inner + k) % n_inner
            spot = block(sent_c, chunk, to, rows_inner)
            remote(spot, spot, send_c.at[chunk, to], recv_c.at[chunk, to], (outer, to)).wait_send()
    everyone(left)
    own.wait()
    everyone(arrived)


def finish(n_all, values, sums, out, rms):
    chunks, _, rows, dim = values.shape
    whole = jnp.sum(jnp.sum(sums[...], axis=0), axis=1, keepdims=True)
    root = jnp.sqrt(whole / (n_all * chunks * rows * dim))
    rms[...] = root
    scale = jnp.broadcast_to(1.0 / root, (8, dim))
    for chunk in range(chunks):
        for c in range(2):
            scaled = values[chunk, c].reshape(-1, 8, dim) * scale[None]
            out[c, pl.ds(chunk, rows, stride=chunks), :] = scaled.reshape(-1, dim)


def shards(n_outer, n_inner, state_vector, gate_matrices):
    dim = gate_matrices.shape[2]
    amp_count = state_vector.shape[3]
    rows = amp_count // dim
    passive = rows // dim
    chunks = passive if (dim // n_outer) % 8 == 0 else 1
    held = pltpu.VMEM((chunks, 2, rows // chunks, dim), jnp.float32)
    n_all = n_outer * n_inner
    dma = pltpu.SemaphoreType.DMA
    vmem = pl.BlockSpec(memory_space=pltpu.VMEM)
    hbm = pl.BlockSpec(memory_space=pltpu.HBM)
    anywhere = pl.BlockSpec(memory_space=pl.ANY)
    values, sums = pl.pallas_call(
        functools.partial(kernel, n_outer, n_inner, chunks),
        out_shape=(
            jax.ShapeDtypeStruct((chunks, 2, rows // chunks, dim), jnp.float32),
            jax.ShapeDtypeStruct((n_all, 1, dim), jnp.float32),
        ),
        in_specs=[hbm, hbm],
        out_specs=(anywhere, anywhere),
        scratch_shapes=[
            pltpu.VMEM((2, rows, dim), jnp.float32),
            pltpu.VMEM(gate_matrices.shape, jnp.float32),
        ]
        + [held] * 5
        + [pltpu.VMEM((1, dim), jnp.float32), dma((5,))]
        + [dma((chunks, n_outer))] * 4
        + [dma((chunks, n_inner))] * 2
        + [dma((n_all,))] * 2,
        compiler_params=pltpu.CompilerParams(
            collective_id=0, has_side_effects=True, vmem_limit_bytes=TRADE_LIMIT
        ),
    )(state_vector.reshape(2, rows, dim), gate_matrices)
    final_state, root = pl.pallas_call(
        functools.partial(finish, n_all),
        out_shape=(
            jax.ShapeDtypeStruct((2, rows, dim), jnp.float32),
            jax.ShapeDtypeStruct((1, 1), jnp.float32),
        ),
        in_specs=[vmem, vmem],
        out_specs=(vmem, vmem),
        compiler_params=pltpu.CompilerParams(vmem_limit_bytes=LIMIT),
    )(values, sums)
    return final_state.reshape(state_vector.shape), root.reshape(())


def relabel(tiles, names, order):
    count = len(names)
    places = [count - 1 - names.index(name) for name in order]
    picked = []
    for at in range(len(tiles)):
        bits = [(at >> (count - 1 - j)) & 1 for j in range(count)]
        picked.append(tiles[sum(bit << place for bit, place in zip(bits, places))])
    return picked


def swap(tiles, names, major, lane):
    step = 1 << (len(names) - 1 - names.index(major))
    lows = [at for at in range(len(tiles)) if not at & step]
    low = jnp.concatenate([tiles[at] for at in lows], axis=0)
    high = jnp.concatenate([tiles[at + step] for at in lows], axis=0)
    size = low.shape[1]
    first = lax.broadcasted_iota(jnp.int32, low.shape, 1) // lane % 2 == 0
    new_low = jnp.where(first, low, pltpu.roll(high, lane, 1))
    new_high = jnp.where(first, pltpu.roll(low, size - lane, 1), high)
    out = list(tiles)
    for j, at in enumerate(lows):
        out[at] = new_low[j * 8 : (j + 1) * 8]
        out[at + step] = new_high[j * 8 : (j + 1) * 8]
    return out


def split(values):
    return [values[at * 8 : (at + 1) * 8] for at in range(values.shape[0] // 8)]


def join(tiles):
    return jnp.concatenate(tiles, axis=0)


def rename(names, old, new):
    return [new if name == old else name for name in names]


def bits(name, count):
    return [name + str(j) for j in reversed(range(count))]


def fast_kernel(
    n_outer, n_inner, state_in, gates_in, held_b, sums,
    state, gates, sent_a, held_a, sent_b, part, fetched,
    send_a, recv_a, send_b, recv_b, send_s, recv_s, own_s,
):
    def fetch(at):
        if at == 0:
            return pltpu.make_async_copy(state_in, state, fetched.at[0])
        return pltpu.make_async_copy(gates_in.at[at - 1], gates.at[at - 1], fetched.at[at])

    dim = gates.shape[2]
    chunks = state.shape[1] // dim
    n_all = n_outer * n_inner
    o_bits, i_bits = n_outer.bit_length() - 1, n_inner.bit_length() - 1
    outer, inner = lax.axis_index("outer"), lax.axis_index("inner")
    me = outer * n_inner + inner

    plane = 2 * n_inner
    levels = n_all // plane
    span = levels // 2
    level, spot = me // plane, me % plane
    side = level // span

    def peer(k):
        j, p = k
        if j < span:
            to = (1 - side) * (levels - 1 - j) + side * j
        else:
            to = side * span + (level + j) % span
        to = to * plane + spot
        for q in range(i_bits + 1):
            if p >> q & 1:
                to = to + (1 - 2 * (spot // 2**q % 2)) * 2**q
        return to // n_inner, to % n_inner

    spots = sorted(range(plane), key=lambda p: (-p.bit_count(), -p))
    across = [(j, p) for j in range(span) for p in spots]
    beside = [(j, p) for j in reversed(range(span, levels)) for p in spots][:-1]
    order = [k for both in zip(across, beside) for k in both] + across[-1:]
    barrier = pltpu.get_barrier_semaphore()
    for k in across + beside:
        pl.semaphore_signal(barrier, inc=1, device_id=peer(k), device_id_type=MESH)
    for at in (0, 1, 4, 2, 3):
        fetch(at).start()

    def remote(src, dst, send, recv, target):
        return pltpu.make_async_remote_copy(
            src_ref=src, dst_ref=dst, send_sem=send, recv_sem=recv,
            device_id=target, device_id_type=MESH,
        )

    def tile(ref, chunk, at):
        return ref.at[chunk, pl.ds(pl.multiple_of(at * 8, 8), 8), :]

    def trade(sent, held, send, recv, chunk, peers):
        for k in peers:
            a, b = peer(k)
            remote(
                tile(sent, chunk, a * n_inner + b), tile(held, chunk, me),
                send.at[chunk], recv.at[chunk], (a, b),
            ).start()

    def keep(sent, held, recv, chunk):
        pltpu.make_async_copy(
            tile(sent, chunk, me), tile(held, chunk, me), recv.at[chunk]
        ).start()

    def arrived(held, send, recv, chunk):
        both = held.at[chunk]
        remote(both, both, send.at[chunk], recv.at[chunk], (outer, inner)).wait_recv()

    def left(sent, send, recv, chunk):
        both = sent.at[chunk, pl.ds(0, (n_all - 1) * 8), :]
        remote(both, both, send.at[chunk], recv.at[chunk], (outer, inner)).wait_send()

    top = dim // 2
    fetch(1).wait()

    def rows0(c):
        return jnp.concatenate(
            [
                gates[0, c, pl.ds(high * top + low, top // 2, stride=2), :]
                for high in range(2)
                for low in range(2)
            ],
            axis=0,
        )

    first = complex_matrix(rows0(0), rows0(1))
    fetch(4).wait()
    real, imag = gates[3, 0], gates[3, 1]
    low = []
    for high in range(2):
        rows = slice(high * top, (high + 1) * top)
        low.append(jnp.concatenate([real[rows], -imag[rows]], axis=1))
        low.append(jnp.concatenate([imag[rows], real[rows]], axis=1))
    low = halves(jnp.concatenate(low, axis=0))
    fetch(0).wait()
    for chunk in range(chunks):
        values = jnp.concatenate(
            [state[c, chunk * dim : (chunk + 1) * dim, :] for c in range(2)], axis=0
        )
        values = product(first, halves(values), ((1,), (0,)))
        wide = jnp.concatenate([values[:dim], values[dim:]], axis=1)
        wide = product(halves(wide), low, ((1,), (1,)))
        tiles = split(jnp.concatenate([wide[:, :dim], wide[:, dim:]], axis=0))
        names = ["b6", "b13", "b7", "b12", "b11"]
        tiles = swap(tiles, names, "b12", dim // 4)
        names = rename(names, "b12", "b5")
        tiles = swap(tiles, names, "b11", dim // 8)
        sent_a[chunk] = join(tiles)
        keep(sent_a, held_a, recv_a, chunk)
        if chunk > 0:
            trade(sent_a, held_a, send_a, recv_a, chunk, order)
            continue
        pl.semaphore_wait(barrier, n_all - 1)
        trade(sent_a, held_a, send_a, recv_a, chunk, order)

    fetch(2).wait()
    second = complex_matrix(gates[1, 0], gates[1, 1])
    fetch(3).wait()
    third = complex_matrix(gates[2, 0], gates[2, 1])
    o_names, i_names = bits("o", o_bits), bits("i", i_bits)
    total = jnp.zeros((1, dim), jnp.float32)
    for chunk in range(chunks):
        arrived(held_a, send_a, recv_a, chunk)
        tiles = split(held_a[chunk])
        names = o_names + i_names
        tiles = swap(tiles, names, "i1", dim // 2)
        names = rename(names, "i1", "c")
        tiles = swap(tiles, names, "i0", dim // 8)
        names = rename(names, "i0", "b11")
        rows = ["c"] + o_names + ["b11"]
        values = product(second, halves(join(relabel(tiles, names, rows))), ((1,), (0,)))
        tiles, names = split(values), rows
        for name, new, lane in (("o2", "i1", 2), ("o1", "b12", 4), ("o0", "i0", 8)):
            tiles = swap(tiles, names, name, dim // lane)
            names = rename(names, name, new)
        rows = ["c"] + i_names + ["b12", "b11"]
        values = product(third, halves(join(relabel(tiles, names, rows))), ((1,), (0,)))
        total = total + jnp.sum(values * values, axis=0, keepdims=True)
        if chunk == chunks - 1:
            part[...] = total
            for k in order:
                remote(part, sums.at[me], send_s, recv_s, peer(k)).start()
            pltpu.make_async_copy(part, sums.at[me], own_s).start()
        tiles, names = split(values), rows
        for name, new, lane in (("c", "o2", 2), ("b12", "o1", 4), ("b11", "o0", 8)):
            tiles = swap(tiles, names, name, dim // lane)
            names = rename(names, name, new)
        sent_b[chunk] = join(relabel(tiles, names, o_names + i_names))
        trade(sent_b, held_b, send_b, recv_b, chunk, order)
        keep(sent_b, held_b, recv_b, chunk)

    for chunk in range(chunks):
        left(sent_a, send_a, recv_a, chunk)
    others = sums.at[pl.ds(0, n_all - 1)]
    remote(others, others, send_s, recv_s, (outer, inner)).wait()
    pltpu.make_async_copy(part, sums.at[me], own_s).wait()
    for chunk in range(chunks):
        arrived(held_b, send_b, recv_b, chunk)
        left(sent_b, send_b, recv_b, chunk)


def fast_finish(n_all, values, sums, out, rms):
    chunks, rows, dim = values.shape
    half = rows // 2
    whole = jnp.sum(jnp.sum(sums[...], axis=0), axis=1, keepdims=True)
    root = jnp.sqrt(whole / (n_all * chunks * half * dim))
    rms[...] = root
    scale = jnp.broadcast_to(1.0 / root, (8, dim))
    for chunk in range(chunks):
        tiles = split(values[chunk])
        names = ["b6", "b13", "b7", "b5", "b4"]
        for name, new, lane in (("b6", "c", 2), ("b5", "b12", 4), ("b4", "b11", 8)):
            tiles = swap(tiles, names, name, dim // lane)
            names = rename(names, name, new)
        tiles = relabel(tiles, names, ["c", "b13", "b12", "b11", "b7"])
        for c in range(2):
            for rest in range(len(tiles) // 2):
                start = chunk * half + rest // 2 * 16 + rest % 2
                out[c, pl.ds(start, 8, stride=2), :] = tiles[c * len(tiles) // 2 + rest] * scale


def fast_shards(n_outer, n_inner, state_vector, gate_matrices):
    dim = gate_matrices.shape[2]
    rows = state_vector.shape[3] // dim
    chunks = rows // dim
    n_all = n_outer * n_inner
    held = pltpu.VMEM((chunks, n_all * 8, dim), jnp.float32)
    dma = pltpu.SemaphoreType.DMA
    vmem = pl.BlockSpec(memory_space=pltpu.VMEM)
    hbm = pl.BlockSpec(memory_space=pltpu.HBM)
    anywhere = pl.BlockSpec(memory_space=pl.ANY)
    values, sums = pl.pallas_call(
        functools.partial(fast_kernel, n_outer, n_inner),
        out_shape=(
            jax.ShapeDtypeStruct((chunks, n_all * 8, dim), jnp.float32),
            jax.ShapeDtypeStruct((n_all, 1, dim), jnp.float32),
        ),
        in_specs=[hbm, hbm],
        out_specs=(anywhere, anywhere),
        scratch_shapes=[
            pltpu.VMEM((2, rows, dim), jnp.float32),
            pltpu.VMEM(gate_matrices.shape, jnp.float32),
        ]
        + [held] * 3
        + [pltpu.VMEM((1, dim), jnp.float32), dma((5,))]
        + [dma((chunks,))] * 4
        + [dma(())] * 3,
        compiler_params=pltpu.CompilerParams(
            collective_id=0, has_side_effects=True, vmem_limit_bytes=TRADE_LIMIT
        ),
    )(state_vector.reshape(2, rows, dim), gate_matrices)
    final_state, root = pl.pallas_call(
        functools.partial(fast_finish, n_all),
        out_shape=(
            jax.ShapeDtypeStruct((2, rows, dim), jnp.float32),
            jax.ShapeDtypeStruct((1, 1), jnp.float32),
        ),
        in_specs=[vmem, vmem],
        out_specs=(vmem, vmem),
        compiler_params=pltpu.CompilerParams(vmem_limit_bytes=LIMIT),
    )(values, sums)
    return final_state.reshape(state_vector.shape), root.reshape(())


def fits(n_outer, n_inner, state_vector, gate_matrices):
    dim = gate_matrices.shape[2]
    rows = state_vector.shape[3] // dim
    return (
        rows == 2 * dim
        and n_outer * n_inner * 8 == 2 * dim
        and dim == n_outer * 16
        and dim == n_inner * 32
    )


def shards_of(n_outer, n_inner, state_vector, gate_matrices):
    run = fast_shards if fits(n_outer, n_inner, state_vector, gate_matrices) else shards
    return run(n_outer, n_inner, state_vector, gate_matrices)


def solution(mesh):
    in_specs = (P(None, "outer", "inner", None), P())
    out_specs = (P(None, "outer", "inner", None), P())
    body = functools.partial(shards_of, mesh.shape["outer"], mesh.shape["inner"])
    return jax.shard_map(body, mesh=mesh, in_specs=in_specs, out_specs=out_specs, check_vma=False)
```

```python
import functools

import jax
import jax.numpy as jnp
from jax import lax
from jax.experimental import pallas as pl
from jax.experimental.pallas import tpu as pltpu
from jax.sharding import PartitionSpec as P

MESH = pl.DeviceIdType.MESH
TRADE_LIMIT = 56_150_000
LIMIT = 16 * 1024 * 1024


def halves(values):
    high = values.astype(jnp.bfloat16)
    low = (values - high.astype(jnp.float32)).astype(jnp.bfloat16)
    return high, low


def product(left, right, dims):
    def one(a, b):
        return lax.dot_general(a, b, (dims, ((), ())), preferred_element_type=jnp.float32)

    return one(left[0], right[0]) + (one(left[0], right[1]) + one(left[1], right[0]))


def complex_matrix(real, imag):
    top = jnp.concatenate([real, -imag], axis=1)
    bottom = jnp.concatenate([imag, real], axis=1)
    return halves(jnp.concatenate([top, bottom], axis=0))


def spread(position, count):
    half, rest = count // 2, position // 2
    return (position % 2) * half + (rest % 2) * (half // 2) + rest // 2


def kernel(
    n_outer, n_inner, chunks, state_in, gates_in, held_c, sums,
    state, gates, sent_a, held_a, sent_b, held_b, sent_c, part, fetched,
    send_a, recv_a, send_b, recv_b, send_c, recv_c, send_s, recv_s,
):
    def fetch(at):
        if at == 0:
            return pltpu.make_async_copy(state_in, state, fetched.at[0])
        return pltpu.make_async_copy(gates_in.at[at - 1], gates.at[at - 1], fetched.at[at])

    for at in (0, 1, 4, 2, 3):
        fetch(at).start()
    dim = gates.shape[2]
    passive = state.shape[1] // dim
    sub = passive // chunks
    step = dim // chunks
    rows_outer = dim // n_outer * sub
    rows_inner = dim // n_inner * sub
    ratio = n_outer // n_inner
    n_all = n_outer * n_inner
    outer, inner = lax.axis_index("outer"), lax.axis_index("inner")
    me = outer * n_inner + inner

    def block(ref, chunk, at, rows):
        return ref.at[chunk, :, pl.ds(pl.multiple_of(at * rows, rows), rows), :]

    def remote(src, dst, send, recv, target):
        return pltpu.make_async_remote_copy(
            src_ref=src, dst_ref=dst, send_sem=send, recv_sem=recv,
            device_id=target, device_id_type=MESH,
        )

    far_first = sorted(range(n_outer), key=lambda k: abs(2 * k - n_outer))

    def everyone(act):
        if n_all > 64:

            def body(k, carry):
                one(act, k // n_inner, k % n_inner)
                return carry

            lax.fori_loop(1, n_all, body, 0)
            return
        for a in far_first:
            for b in range(n_inner):
                if a or b:
                    one(act, a, b)

    def one(act, a, b):
        ahead = ((outer + a) % n_outer, (inner + b) % n_inner)
        behind = ((outer + n_outer - a) % n_outer, (inner + n_inner - b) % n_inner)
        act(a * n_inner + b, ahead, behind)

    barrier = pltpu.get_barrier_semaphore()

    for k in range(1, n_outer):
        pl.semaphore_signal(
            barrier, inc=1, device_id=((outer + k) % n_outer, inner), device_id_type=MESH
        )
    for k in range(1, n_inner):
        pl.semaphore_signal(
            barrier, inc=1, device_id=(outer, (inner + k) % n_inner), device_id_type=MESH
        )

    def load(ref, chunk):
        return jnp.concatenate(
            [
                jnp.concatenate(
                    [ref[chunk, c, pl.ds(b, dim, stride=sub), :] for b in range(sub)], axis=1
                )
                for c in range(2)
            ],
            axis=0,
        )

    def store(ref, chunk, values):
        for c in range(2):
            for b in range(sub):
                ref[chunk, c, pl.ds(b, dim, stride=sub), :] = values[
                    c * dim : (c + 1) * dim, b * dim : (b + 1) * dim
                ]

    def low_gate(values):
        rows = values.shape[0] // 2
        matrix = complex_matrix(gates[3, 0], gates[3, 1])
        columns = []
        for b in range(values.shape[1] // dim):
            both = values[:, b * dim : (b + 1) * dim]
            wide = jnp.concatenate([both[:rows], both[rows:]], axis=1)
            wide = product(halves(wide), matrix, ((1,), (1,)))
            columns.append(jnp.concatenate([wide[:, :dim], wide[:, dim:]], axis=0))
        return jnp.concatenate(columns, axis=1)

    fetch(0).wait()
    fetch(1).wait()
    first = halves(
        jnp.concatenate(
            [
                jnp.concatenate(
                    [state[c, w * dim : (w + 1) * dim, :] for w in range(passive)], axis=1
                )
                for c in range(2)
            ],
            axis=0,
        )
    )

    def trade_a(chunk):
        for k in far_first[:-1]:
            to = (outer + k) % n_outer
            remote(
                block(sent_a, chunk, spread(to, n_outer), rows_outer),
                block(held_a, chunk, outer, rows_outer),
                send_a.at[chunk, to], recv_a.at[chunk, outer], (to, inner),
            ).start()
        pltpu.make_async_copy(
            block(sent_a, chunk, spread(outer, n_outer), rows_outer),
            block(held_a, chunk, outer, rows_outer),
            recv_a.at[chunk, outer],
        ).start()

    for chunk in range(chunks):
        pick = pl.ds(chunk, step, stride=chunks)
        matrix = complex_matrix(gates[0, 0, pick, :], gates[0, 1, pick, :])
        values = product(matrix, first, ((1,), (0,)))
        if chunk > 0:
            if chunk == 1:
                fetch(4).wait()
            values = low_gate(values)
        for c in range(2):
            for w in range(passive):
                sent_a[chunk, c, w * step : (w + 1) * step, :] = values[
                    c * step : (c + 1) * step, w * dim : (w + 1) * dim
                ]
        if chunk == 0:
            pl.semaphore_wait(barrier, n_outer + n_inner - 2)
        trade_a(chunk)

    fetch(2).wait()
    matrix = complex_matrix(gates[1, 0], gates[1, 1])
    mine = spread(outer, n_outer)
    column, within = mine // ratio, mine % ratio
    slot = inner * ratio + within
    for chunk in range(chunks):
        for k in range(n_outer):
            spot = block(held_a, chunk, k, rows_outer)
            remote(spot, spot, send_a.at[chunk, k], recv_a.at[chunk, k], (outer, inner)).wait_recv()
        values = halves(load(held_a, chunk))
        store(sent_b, chunk, product(matrix, values, ((1,), (0,))))
        for k in far_first:
            to = (outer + k) % n_outer
            src = block(sent_b, chunk, to, rows_outer)
            dst = block(held_b, chunk, slot, rows_outer)
            copy = remote(
                src, dst, send_b.at[chunk, to], recv_b.at[chunk, slot], (to, column)
            )
            if k > 0:
                copy.start()
            else:
                pl.when(column != inner)(copy.start)
                pl.when(column == inner)(
                    pltpu.make_async_copy(src, dst, recv_b.at[chunk, slot]).start
                )

    fetch(3).wait()
    matrix = complex_matrix(gates[2, 0], gates[2, 1])
    total = jnp.zeros((1, dim), jnp.float32)
    own = pltpu.make_async_copy(part, sums.at[me], recv_s.at[0])

    def share(k, ahead, behind):
        remote(part, sums.at[me], send_s.at[k], recv_s.at[k], ahead).start()

    for chunk in range(chunks):
        for k in range(n_outer):
            spot = block(held_b, chunk, k, rows_outer)
            remote(spot, spot, send_b.at[chunk, k], recv_b.at[chunk, k], (outer, inner)).wait_recv()
        values = product(matrix, halves(load(held_b, chunk)), ((1,), (0,)))
        if chunk == 0:
            if chunks == 1:
                fetch(4).wait()
            values = low_gate(values)
        for b in range(sub):
            piece = values[:, b * dim : (b + 1) * dim]
            total = total + jnp.sum(piece * piece, axis=0, keepdims=True)
        if chunk == chunks - 1:
            part[...] = total
            everyone(share)
            own.start()
        store(sent_c, chunk, values)
        for k in range(1, n_inner):
            to = (inner + k) % n_inner
            remote(
                block(sent_c, chunk, to, rows_inner),
                block(held_c, chunk, inner, rows_inner),
                send_c.at[chunk, to], recv_c.at[chunk, inner], (outer, to),
            ).start()
        pltpu.make_async_copy(
            block(sent_c, chunk, inner, rows_inner),
            block(held_c, chunk, inner, rows_inner),
            recv_c.at[chunk, inner],
        ).start()

    def arrived(k, ahead, behind):
        spot = sums.at[behind[0] * n_inner + behind[1]]
        remote(part, spot, send_s.at[k], recv_s.at[k], ahead).wait_recv()

    def left(k, ahead, behind):
        remote(part, sums.at[me], send_s.at[k], recv_s.at[k], ahead).wait_send()

    for chunk in range(chunks):
        for k in range(n_inner):
            spot = block(held_c, chunk, k, rows_inner)
            remote(spot, spot, send_c.at[chunk, k], recv_c.at[chunk, k], (outer, inner)).wait_recv()

    for chunk in range(chunks):
        for k in range(1, n_outer):
            to = (outer + k) % n_outer
            spot = block(sent_a, chunk, to, rows_outer)
            remote(spot, spot, send_a.at[chunk, to], recv_a.at[chunk, to], (to, inner)).wait_send()
        for k in range(n_outer):
            to = (outer + k) % n_outer
            spot = block(sent_b, chunk, to, rows_outer)
            copy = remote(spot, spot, send_b.at[chunk, to], recv_b.at[chunk, to], (to, column))
            if k > 0:
                copy.wait_send()
            else:
                pl.when(column != inner)(copy.wait_send)
        for k in range(1, n_inner):
            to = (inner + k) % n_inner
            spot = block(sent_c, chunk, to, rows_inner)
            remote(spot, spot, send_c.at[chunk, to], recv_c.at[chunk, to], (outer, to)).wait_send()
    everyone(left)
    own.wait()
    everyone(arrived)


def finish(n_all, values, sums, out, rms):
    chunks, _, rows, dim = values.shape
    whole = jnp.sum(jnp.sum(sums[...], axis=0), axis=1, keepdims=True)
    root = jnp.sqrt(whole / (n_all * chunks * rows * dim))
    rms[...] = root
    scale = jnp.broadcast_to(1.0 / root, (8, dim))
    for chunk in range(chunks):
        for c in range(2):
            scaled = values[chunk, c].reshape(-1, 8, dim) * scale[None]
            out[c, pl.ds(chunk, rows, stride=chunks), :] = scaled.reshape(-1, dim)


def shards(n_outer, n_inner, state_vector, gate_matrices):
    dim = gate_matrices.shape[2]
    amp_count = state_vector.shape[3]
    rows = amp_count // dim
    passive = rows // dim
    chunks = passive if (dim // n_outer) % 8 == 0 else 1
    held = pltpu.VMEM((chunks, 2, rows // chunks, dim), jnp.float32)
    n_all = n_outer * n_inner
    dma = pltpu.SemaphoreType.DMA
    vmem = pl.BlockSpec(memory_space=pltpu.VMEM)
    hbm = pl.BlockSpec(memory_space=pltpu.HBM)
    anywhere = pl.BlockSpec(memory_space=pl.ANY)
    values, sums = pl.pallas_call(
        functools.partial(kernel, n_outer, n_inner, chunks),
        out_shape=(
            jax.ShapeDtypeStruct((chunks, 2, rows // chunks, dim), jnp.float32),
            jax.ShapeDtypeStruct((n_all, 1, dim), jnp.float32),
        ),
        in_specs=[hbm, hbm],
        out_specs=(anywhere, anywhere),
        scratch_shapes=[
            pltpu.VMEM((2, rows, dim), jnp.float32),
            pltpu.VMEM(gate_matrices.shape, jnp.float32),
        ]
        + [held] * 5
        + [pltpu.VMEM((1, dim), jnp.float32), dma((5,))]
        + [dma((chunks, n_outer))] * 4
        + [dma((chunks, n_inner))] * 2
        + [dma((n_all,))] * 2,
        compiler_params=pltpu.CompilerParams(
            collective_id=0, has_side_effects=True, vmem_limit_bytes=TRADE_LIMIT
        ),
    )(state_vector.reshape(2, rows, dim), gate_matrices)
    final_state, root = pl.pallas_call(
        functools.partial(finish, n_all),
        out_shape=(
            jax.ShapeDtypeStruct((2, rows, dim), jnp.float32),
            jax.ShapeDtypeStruct((1, 1), jnp.float32),
        ),
        in_specs=[vmem, vmem],
        out_specs=(vmem, vmem),
        compiler_params=pltpu.CompilerParams(vmem_limit_bytes=LIMIT),
    )(values, sums)
    return final_state.reshape(state_vector.shape), root.reshape(())


def relabel(tiles, names, order):
    count = len(names)
    places = [count - 1 - names.index(name) for name in order]
    picked = []
    for at in range(len(tiles)):
        bits = [(at >> (count - 1 - j)) & 1 for j in range(count)]
        picked.append(tiles[sum(bit << place for bit, place in zip(bits, places))])
    return picked


def lane_bit(size, lane):
    return lax.broadcasted_iota(jnp.int32, (8, size), 1) // lane % 2 == 1


def swap(tiles, names, major, lane):
    step = 1 << (len(names) - 1 - names.index(major))
    size = tiles[0].shape[1]
    second = lane_bit(size, lane)
    out = list(tiles)
    for at in range(len(tiles)):
        if not at & step:
            low, high = tiles[at], tiles[at + step]
            out[at] = jnp.where(second, pltpu.roll(high, lane, 1), low)
            out[at + step] = jnp.where(second, high, pltpu.roll(low, size - lane, 1))
    return out


def turn(tiles, names, majors, rolled=False, roll=True):
    count, size = len(majors), tiles[0].shape[1]
    many, group = 1 << count, size >> count
    steps = [1 << (len(names) - 1 - names.index(name)) for name in majors]
    places = [
        sum(step for j, step in enumerate(steps) if at >> (count - 1 - j) & 1)
        for at in range(many)
    ]
    picks = [lane_bit(size, group << j) for j in range(count)]
    out = list(tiles)
    for base in range(len(tiles)):
        if base & sum(steps):
            continue
        held = [tiles[base + place] for place in places]
        if not rolled:
            held = [held[0]] + [pltpu.roll(held[j], j * group, 1) for j in range(1, many)]
        held = [held[-j % many] for j in range(many)]
        for j, pick in enumerate(picks):
            held = [jnp.where(pick, held[(at - 2**j) % many], held[at]) for at in range(many)]
        for at, place in enumerate(places):
            turned = roll and at > 0
            out[base + place] = pltpu.roll(held[at], size - at * group, 1) if turned else held[at]
    return out


def wide_product(left, right):
    def one(a, b):
        return lax.dot_general(a, b, (((1,), (0,)), ((), ())), preferred_element_type=jnp.float32)

    count = right[0].shape[1]
    both = one(left[0], jnp.concatenate(right, axis=1))
    return both[:, :count] + (both[:, count:] + one(left[1], right[0]))


def split(values):
    return [values[at * 8 : (at + 1) * 8] for at in range(values.shape[0] // 8)]


def join(tiles):
    return jnp.concatenate(tiles, axis=0)


def rename(names, old, new):
    return [new if name == old else name for name in names]


def bits(name, count):
    return [name + str(j) for j in reversed(range(count))]


def fast_kernel(
    n_outer, n_inner, state_in, gates_in, held_b, sums,
    state, gates, sent_a, held_a, sent_b, part, fetched,
    send_a, recv_a, send_b, recv_b, send_s, recv_s, own_s,
):
    def fetch(at):
        if at == 0:
            return pltpu.make_async_copy(state_in, state, fetched.at[0])
        return pltpu.make_async_copy(gates_in.at[at - 1], gates.at[at - 1], fetched.at[at])

    dim = gates.shape[2]
    chunks = state.shape[1] // dim
    n_all = n_outer * n_inner
    o_bits, i_bits = n_outer.bit_length() - 1, n_inner.bit_length() - 1
    outer, inner = lax.axis_index("outer"), lax.axis_index("inner")
    me = outer * n_inner + inner

    plane = 2 * n_inner
    levels = n_all // plane
    span = levels // 2
    level, spot = me // plane, me % plane
    side = level // span

    def peer(k):
        j, p = k
        if j < span:
            to = (1 - side) * (levels - 1 - j) + side * j
        else:
            to = side * span + (level + j) % span
        to = to * plane + spot
        for q in range(i_bits + 1):
            if p >> q & 1:
                to = to + (1 - 2 * (spot // 2**q % 2)) * 2**q
        return to // n_inner, to % n_inner

    spots = sorted(range(plane), key=lambda p: (-p.bit_count(), -p))
    across = [(j, p) for j in range(span) for p in spots]
    beside = [(j, p) for j in reversed(range(span, levels)) for p in spots][:-1]
    order = [k for both in zip(across, beside) for k in both] + across[-1:]
    barrier = pltpu.get_barrier_semaphore()
    for k in across + beside:
        pl.semaphore_signal(barrier, inc=1, device_id=peer(k), device_id_type=MESH)
    for at in (0, 1, 4, 2, 3):
        fetch(at).start()

    def remote(src, dst, send, recv, target):
        return pltpu.make_async_remote_copy(
            src_ref=src, dst_ref=dst, send_sem=send, recv_sem=recv,
            device_id=target, device_id_type=MESH,
        )

    def tile(ref, chunk, at):
        return ref.at[chunk, pl.ds(pl.multiple_of(at * 8, 8), 8), :]

    def trade(sent, held, send, recv, chunk, peers):
        for k in peers:
            a, b = peer(k)
            remote(
                tile(sent, chunk, a * n_inner + b), tile(held, chunk, me),
                send.at[chunk], recv.at[chunk], (a, b),
            ).start()

    def keep(sent, held, recv, chunk):
        pltpu.make_async_copy(
            tile(sent, chunk, me), tile(held, chunk, me), recv.at[chunk]
        ).start()

    def arrived(held, send, recv, chunk):
        both = held.at[chunk]
        remote(both, both, send.at[chunk], recv.at[chunk], (outer, inner)).wait_recv()

    def left(sent, send, recv, chunk):
        both = sent.at[chunk, pl.ds(0, (n_all - 1) * 8), :]
        remote(both, both, send.at[chunk], recv.at[chunk], (outer, inner)).wait_send()

    top = dim // 2
    fetch(1).wait()

    def rows0(c):
        return jnp.concatenate(
            [
                gates[0, c, pl.ds(high * top + low, top // 2, stride=2), :]
                for high in range(2)
                for low in range(2)
            ],
            axis=0,
        )

    first = complex_matrix(rows0(0), rows0(1))
    fetch(4).wait()
    real, imag = gates[3, 0], gates[3, 1]
    low = []
    for high in range(2):
        rows = slice(high * top, (high + 1) * top)
        low.append(jnp.concatenate([real[rows], -imag[rows]], axis=1))
        low.append(jnp.concatenate([imag[rows], real[rows]], axis=1))
    low = halves(jnp.concatenate(low, axis=0))
    fetch(0).wait()
    for chunk in range(chunks):
        values = jnp.concatenate(
            [state[c, chunk * dim : (chunk + 1) * dim, :] for c in range(2)], axis=0
        )
        values = product(first, halves(values), ((1,), (0,)))
        wide = jnp.concatenate([values[:dim], values[dim:]], axis=1)
        wide = product(halves(wide), low, ((1,), (1,)))
        tiles = split(jnp.concatenate([wide[:, :dim], wide[:, dim:]], axis=0))
        names = ["b6", "b13", "b7", "b12", "b11"]
        tiles = swap(tiles, names, "b11", dim // 4)
        names = rename(names, "b11", "b5")
        tiles = swap(tiles, names, "b12", dim // 8)
        names = rename(names, "b12", "b4")
        tiles = relabel(tiles, names, ["b6", "b13", "b7", "b5", "b4"])
        sent_a[chunk] = pltpu.roll(join(tiles), inner * (dim // n_inner), 1)
        keep(sent_a, held_a, recv_a, chunk)
        if chunk > 0:
            trade(sent_a, held_a, send_a, recv_a, chunk, order)
            continue
        pl.semaphore_wait(barrier, n_all - 1)
        trade(sent_a, held_a, send_a, recv_a, chunk, order)

    fetch(2).wait()
    second = complex_matrix(gates[1, 0], gates[1, 1])
    fetch(3).wait()
    third = complex_matrix(gates[2, 0], gates[2, 1])
    o_names, i_names = bits("o", o_bits), bits("i", i_bits)
    total = jnp.zeros((1, dim), jnp.float32)
    for chunk in range(chunks):
        arrived(held_a, send_a, recv_a, chunk)
        tiles = turn(split(held_a[chunk]), o_names + i_names, i_names, rolled=True)
        names = o_names + ["c", "b11"]
        rows = ["c"] + o_names + ["b11"]
        values = wide_product(second, halves(join(relabel(tiles, names, rows))))
        tiles = turn(split(values), rows, o_names)
        names = ["c"] + i_names + ["b12", "b11"]
        rows = ["c"] + i_names + ["b12", "b11"]
        values = wide_product(third, halves(join(relabel(tiles, names, rows))))
        total = total + jnp.sum(values * values, axis=0, keepdims=True)
        if chunk == chunks - 1:
            part[...] = total
            for k in order:
                remote(part, sums.at[me], send_s, recv_s, peer(k)).start()
            pltpu.make_async_copy(part, sums.at[me], own_s).start()
        tiles = turn(split(values), rows, ["c", "b11", "b12"], roll=False)
        names = ["o2"] + i_names + ["o0", "o1"]
        sent_b[chunk] = join(relabel(tiles, names, o_names + i_names))
        trade(sent_b, held_b, send_b, recv_b, chunk, order)
        keep(sent_b, held_b, recv_b, chunk)

    for chunk in range(chunks):
        left(sent_a, send_a, recv_a, chunk)
    others = sums.at[pl.ds(0, n_all - 1)]
    remote(others, others, send_s, recv_s, (outer, inner)).wait()
    pltpu.make_async_copy(part, sums.at[me], own_s).wait()
    for chunk in range(chunks):
        arrived(held_b, send_b, recv_b, chunk)
        left(sent_b, send_b, recv_b, chunk)


def fast_finish(n_all, values, sums, out, rms):
    chunks, rows, dim = values.shape
    half = rows // 2
    whole = jnp.sum(jnp.sum(sums[...], axis=0), axis=1, keepdims=True)
    root = jnp.sqrt(whole / (n_all * chunks * half * dim))
    rms[...] = root
    scale = jnp.broadcast_to(1.0 / root, (8, dim))
    outer = lax.axis_index("outer")
    turned = [(dim + (j - outer) * (dim // 8)) % dim for j in range(8)]
    for chunk in range(chunks):
        names = ["b6", "b13", "b7", "b5", "b4"]
        tiles = split(values[chunk])
        for at in range(len(tiles)):
            ahead = 4 * (at >> 4) + (at & 3)
            tiles[at] = pltpu.roll(tiles[at], turned[ahead], 1)
        tiles = turn(tiles, names, ["b6", "b5", "b4"], rolled=True)
        names = ["c", "b13", "b7", "b11", "b12"]
        tiles = relabel(tiles, names, ["c", "b13", "b12", "b11", "b7"])
        for c in range(2):
            for rest in range(len(tiles) // 2):
                start = chunk * half + rest // 2 * 16 + rest % 2
                out[c, pl.ds(start, 8, stride=2), :] = tiles[c * len(tiles) // 2 + rest] * scale


def fast_shards(n_outer, n_inner, state_vector, gate_matrices):
    dim = gate_matrices.shape[2]
    rows = state_vector.shape[3] // dim
    chunks = rows // dim
    n_all = n_outer * n_inner
    held = pltpu.VMEM((chunks, n_all * 8, dim), jnp.float32)
    dma = pltpu.SemaphoreType.DMA
    vmem = pl.BlockSpec(memory_space=pltpu.VMEM)
    hbm = pl.BlockSpec(memory_space=pltpu.HBM)
    anywhere = pl.BlockSpec(memory_space=pl.ANY)
    values, sums = pl.pallas_call(
        functools.partial(fast_kernel, n_outer, n_inner),
        out_shape=(
            jax.ShapeDtypeStruct((chunks, n_all * 8, dim), jnp.float32),
            jax.ShapeDtypeStruct((n_all, 1, dim), jnp.float32),
        ),
        in_specs=[hbm, hbm],
        out_specs=(anywhere, anywhere),
        scratch_shapes=[
            pltpu.VMEM((2, rows, dim), jnp.float32),
            pltpu.VMEM(gate_matrices.shape, jnp.float32),
        ]
        + [held] * 3
        + [pltpu.VMEM((1, dim), jnp.float32), dma((5,))]
        + [dma((chunks,))] * 4
        + [dma(())] * 3,
        compiler_params=pltpu.CompilerParams(
            collective_id=0, has_side_effects=True, vmem_limit_bytes=TRADE_LIMIT
        ),
    )(state_vector.reshape(2, rows, dim), gate_matrices)
    final_state, root = pl.pallas_call(
        functools.partial(fast_finish, n_all),
        out_shape=(
            jax.ShapeDtypeStruct((2, rows, dim), jnp.float32),
            jax.ShapeDtypeStruct((1, 1), jnp.float32),
        ),
        in_specs=[vmem, vmem],
        out_specs=(vmem, vmem),
        compiler_params=pltpu.CompilerParams(vmem_limit_bytes=LIMIT),
    )(values, sums)
    return final_state.reshape(state_vector.shape), root.reshape(())


def fits(n_outer, n_inner, state_vector, gate_matrices):
    dim = gate_matrices.shape[2]
    rows = state_vector.shape[3] // dim
    return (
        rows == 2 * dim
        and n_outer * n_inner * 8 == 2 * dim
        and dim == n_outer * 16
        and dim == n_inner * 32
    )


def shards_of(n_outer, n_inner, state_vector, gate_matrices):
    run = fast_shards if fits(n_outer, n_inner, state_vector, gate_matrices) else shards
    return run(n_outer, n_inner, state_vector, gate_matrices)


def solution(mesh):
    in_specs = (P(None, "outer", "inner", None), P())
    out_specs = (P(None, "outer", "inner", None), P())
    body = functools.partial(shards_of, mesh.shape["outer"], mesh.shape["inner"])
    return jax.shard_map(body, mesh=mesh, in_specs=in_specs, out_specs=out_specs, check_vma=False)
```

```python
import functools

import jax
import jax.numpy as jnp
from jax import lax
from jax.experimental import pallas as pl
from jax.experimental.pallas import tpu as pltpu
from jax.sharding import PartitionSpec as P

MESH = pl.DeviceIdType.MESH
TRADE_LIMIT = 56_150_000
LIMIT = 16 * 1024 * 1024


def halves(values):
    high = values.astype(jnp.bfloat16)
    low = (values - high.astype(jnp.float32)).astype(jnp.bfloat16)
    return high, low


def product(left, right, dims):
    def one(a, b):
        return lax.dot_general(a, b, (dims, ((), ())), preferred_element_type=jnp.float32)

    return one(left[0], right[0]) + (one(left[0], right[1]) + one(left[1], right[0]))


def complex_matrix(real, imag):
    top = jnp.concatenate([real, -imag], axis=1)
    bottom = jnp.concatenate([imag, real], axis=1)
    return halves(jnp.concatenate([top, bottom], axis=0))


def spread(position, count):
    half, rest = count // 2, position // 2
    return (position % 2) * half + (rest % 2) * (half // 2) + rest // 2


def kernel(
    n_outer, n_inner, chunks, state_in, gates_in, held_c, sums,
    state, gates, sent_a, held_a, sent_b, held_b, sent_c, part, fetched,
    send_a, recv_a, send_b, recv_b, send_c, recv_c, send_s, recv_s,
):
    def fetch(at):
        if at == 0:
            return pltpu.make_async_copy(state_in, state, fetched.at[0])
        return pltpu.make_async_copy(gates_in.at[at - 1], gates.at[at - 1], fetched.at[at])

    for at in (0, 1, 4, 2, 3):
        fetch(at).start()
    dim = gates.shape[2]
    passive = state.shape[1] // dim
    sub = passive // chunks
    step = dim // chunks
    rows_outer = dim // n_outer * sub
    rows_inner = dim // n_inner * sub
    ratio = n_outer // n_inner
    n_all = n_outer * n_inner
    outer, inner = lax.axis_index("outer"), lax.axis_index("inner")
    me = outer * n_inner + inner

    def block(ref, chunk, at, rows):
        return ref.at[chunk, :, pl.ds(pl.multiple_of(at * rows, rows), rows), :]

    def remote(src, dst, send, recv, target):
        return pltpu.make_async_remote_copy(
            src_ref=src, dst_ref=dst, send_sem=send, recv_sem=recv,
            device_id=target, device_id_type=MESH,
        )

    far_first = sorted(range(n_outer), key=lambda k: abs(2 * k - n_outer))

    def everyone(act):
        if n_all > 64:

            def body(k, carry):
                one(act, k // n_inner, k % n_inner)
                return carry

            lax.fori_loop(1, n_all, body, 0)
            return
        for a in far_first:
            for b in range(n_inner):
                if a or b:
                    one(act, a, b)

    def one(act, a, b):
        ahead = ((outer + a) % n_outer, (inner + b) % n_inner)
        behind = ((outer + n_outer - a) % n_outer, (inner + n_inner - b) % n_inner)
        act(a * n_inner + b, ahead, behind)

    barrier = pltpu.get_barrier_semaphore()

    for k in range(1, n_outer):
        pl.semaphore_signal(
            barrier, inc=1, device_id=((outer + k) % n_outer, inner), device_id_type=MESH
        )
    for k in range(1, n_inner):
        pl.semaphore_signal(
            barrier, inc=1, device_id=(outer, (inner + k) % n_inner), device_id_type=MESH
        )

    def load(ref, chunk):
        return jnp.concatenate(
            [
                jnp.concatenate(
                    [ref[chunk, c, pl.ds(b, dim, stride=sub), :] for b in range(sub)], axis=1
                )
                for c in range(2)
            ],
            axis=0,
        )

    def store(ref, chunk, values):
        for c in range(2):
            for b in range(sub):
                ref[chunk, c, pl.ds(b, dim, stride=sub), :] = values[
                    c * dim : (c + 1) * dim, b * dim : (b + 1) * dim
                ]

    def low_gate(values):
        rows = values.shape[0] // 2
        matrix = complex_matrix(gates[3, 0], gates[3, 1])
        columns = []
        for b in range(values.shape[1] // dim):
            both = values[:, b * dim : (b + 1) * dim]
            wide = jnp.concatenate([both[:rows], both[rows:]], axis=1)
            wide = product(halves(wide), matrix, ((1,), (1,)))
            columns.append(jnp.concatenate([wide[:, :dim], wide[:, dim:]], axis=0))
        return jnp.concatenate(columns, axis=1)

    fetch(0).wait()
    fetch(1).wait()
    first = halves(
        jnp.concatenate(
            [
                jnp.concatenate(
                    [state[c, w * dim : (w + 1) * dim, :] for w in range(passive)], axis=1
                )
                for c in range(2)
            ],
            axis=0,
        )
    )

    def trade_a(chunk):
        for k in far_first[:-1]:
            to = (outer + k) % n_outer
            remote(
                block(sent_a, chunk, spread(to, n_outer), rows_outer),
                block(held_a, chunk, outer, rows_outer),
                send_a.at[chunk, to], recv_a.at[chunk, outer], (to, inner),
            ).start()
        pltpu.make_async_copy(
            block(sent_a, chunk, spread(outer, n_outer), rows_outer),
            block(held_a, chunk, outer, rows_outer),
            recv_a.at[chunk, outer],
        ).start()

    for chunk in range(chunks):
        pick = pl.ds(chunk, step, stride=chunks)
        matrix = complex_matrix(gates[0, 0, pick, :], gates[0, 1, pick, :])
        values = product(matrix, first, ((1,), (0,)))
        if chunk > 0:
            if chunk == 1:
                fetch(4).wait()
            values = low_gate(values)
        for c in range(2):
            for w in range(passive):
                sent_a[chunk, c, w * step : (w + 1) * step, :] = values[
                    c * step : (c + 1) * step, w * dim : (w + 1) * dim
                ]
        if chunk == 0:
            pl.semaphore_wait(barrier, n_outer + n_inner - 2)
        trade_a(chunk)

    fetch(2).wait()
    matrix = complex_matrix(gates[1, 0], gates[1, 1])
    mine = spread(outer, n_outer)
    column, within = mine // ratio, mine % ratio
    slot = inner * ratio + within
    for chunk in range(chunks):
        for k in range(n_outer):
            spot = block(held_a, chunk, k, rows_outer)
            remote(spot, spot, send_a.at[chunk, k], recv_a.at[chunk, k], (outer, inner)).wait_recv()
        values = halves(load(held_a, chunk))
        store(sent_b, chunk, product(matrix, values, ((1,), (0,))))
        for k in far_first:
            to = (outer + k) % n_outer
            src = block(sent_b, chunk, to, rows_outer)
            dst = block(held_b, chunk, slot, rows_outer)
            copy = remote(
                src, dst, send_b.at[chunk, to], recv_b.at[chunk, slot], (to, column)
            )
            if k > 0:
                copy.start()
            else:
                pl.when(column != inner)(copy.start)
                pl.when(column == inner)(
                    pltpu.make_async_copy(src, dst, recv_b.at[chunk, slot]).start
                )

    fetch(3).wait()
    matrix = complex_matrix(gates[2, 0], gates[2, 1])
    total = jnp.zeros((1, dim), jnp.float32)
    own = pltpu.make_async_copy(part, sums.at[me], recv_s.at[0])

    def share(k, ahead, behind):
        remote(part, sums.at[me], send_s.at[k], recv_s.at[k], ahead).start()

    for chunk in range(chunks):
        for k in range(n_outer):
            spot = block(held_b, chunk, k, rows_outer)
            remote(spot, spot, send_b.at[chunk, k], recv_b.at[chunk, k], (outer, inner)).wait_recv()
        values = product(matrix, halves(load(held_b, chunk)), ((1,), (0,)))
        if chunk == 0:
            if chunks == 1:
                fetch(4).wait()
            values = low_gate(values)
        for b in range(sub):
            piece = values[:, b * dim : (b + 1) * dim]
            total = total + jnp.sum(piece * piece, axis=0, keepdims=True)
        if chunk == chunks - 1:
            part[...] = total
            everyone(share)
            own.start()
        store(sent_c, chunk, values)
        for k in range(1, n_inner):
            to = (inner + k) % n_inner
            remote(
                block(sent_c, chunk, to, rows_inner),
                block(held_c, chunk, inner, rows_inner),
                send_c.at[chunk, to], recv_c.at[chunk, inner], (outer, to),
            ).start()
        pltpu.make_async_copy(
            block(sent_c, chunk, inner, rows_inner),
            block(held_c, chunk, inner, rows_inner),
            recv_c.at[chunk, inner],
        ).start()

    def arrived(k, ahead, behind):
        spot = sums.at[behind[0] * n_inner + behind[1]]
        remote(part, spot, send_s.at[k], recv_s.at[k], ahead).wait_recv()

    def left(k, ahead, behind):
        remote(part, sums.at[me], send_s.at[k], recv_s.at[k], ahead).wait_send()

    for chunk in range(chunks):
        for k in range(n_inner):
            spot = block(held_c, chunk, k, rows_inner)
            remote(spot, spot, send_c.at[chunk, k], recv_c.at[chunk, k], (outer, inner)).wait_recv()

    for chunk in range(chunks):
        for k in range(1, n_outer):
            to = (outer + k) % n_outer
            spot = block(sent_a, chunk, to, rows_outer)
            remote(spot, spot, send_a.at[chunk, to], recv_a.at[chunk, to], (to, inner)).wait_send()
        for k in range(n_outer):
            to = (outer + k) % n_outer
            spot = block(sent_b, chunk, to, rows_outer)
            copy = remote(spot, spot, send_b.at[chunk, to], recv_b.at[chunk, to], (to, column))
            if k > 0:
                copy.wait_send()
            else:
                pl.when(column != inner)(copy.wait_send)
        for k in range(1, n_inner):
            to = (inner + k) % n_inner
            spot = block(sent_c, chunk, to, rows_inner)
            remote(spot, spot, send_c.at[chunk, to], recv_c.at[chunk, to], (outer, to)).wait_send()
    everyone(left)
    own.wait()
    everyone(arrived)


def finish(n_all, values, sums, out, rms):
    chunks, _, rows, dim = values.shape
    whole = jnp.sum(jnp.sum(sums[...], axis=0), axis=1, keepdims=True)
    root = jnp.sqrt(whole / (n_all * chunks * rows * dim))
    rms[...] = root
    scale = jnp.broadcast_to(1.0 / root, (8, dim))
    for chunk in range(chunks):
        for c in range(2):
            scaled = values[chunk, c].reshape(-1, 8, dim) * scale[None]
            out[c, pl.ds(chunk, rows, stride=chunks), :] = scaled.reshape(-1, dim)


def shards(n_outer, n_inner, state_vector, gate_matrices):
    dim = gate_matrices.shape[2]
    amp_count = state_vector.shape[3]
    rows = amp_count // dim
    passive = rows // dim
    chunks = passive if (dim // n_outer) % 8 == 0 else 1
    held = pltpu.VMEM((chunks, 2, rows // chunks, dim), jnp.float32)
    n_all = n_outer * n_inner
    dma = pltpu.SemaphoreType.DMA
    vmem = pl.BlockSpec(memory_space=pltpu.VMEM)
    hbm = pl.BlockSpec(memory_space=pltpu.HBM)
    anywhere = pl.BlockSpec(memory_space=pl.ANY)
    values, sums = pl.pallas_call(
        functools.partial(kernel, n_outer, n_inner, chunks),
        out_shape=(
            jax.ShapeDtypeStruct((chunks, 2, rows // chunks, dim), jnp.float32),
            jax.ShapeDtypeStruct((n_all, 1, dim), jnp.float32),
        ),
        in_specs=[hbm, hbm],
        out_specs=(anywhere, anywhere),
        scratch_shapes=[
            pltpu.VMEM((2, rows, dim), jnp.float32),
            pltpu.VMEM(gate_matrices.shape, jnp.float32),
        ]
        + [held] * 5
        + [pltpu.VMEM((1, dim), jnp.float32), dma((5,))]
        + [dma((chunks, n_outer))] * 4
        + [dma((chunks, n_inner))] * 2
        + [dma((n_all,))] * 2,
        compiler_params=pltpu.CompilerParams(
            collective_id=0, has_side_effects=True, vmem_limit_bytes=TRADE_LIMIT
        ),
    )(state_vector.reshape(2, rows, dim), gate_matrices)
    final_state, root = pl.pallas_call(
        functools.partial(finish, n_all),
        out_shape=(
            jax.ShapeDtypeStruct((2, rows, dim), jnp.float32),
            jax.ShapeDtypeStruct((1, 1), jnp.float32),
        ),
        in_specs=[vmem, vmem],
        out_specs=(vmem, vmem),
        compiler_params=pltpu.CompilerParams(vmem_limit_bytes=LIMIT),
    )(values, sums)
    return final_state.reshape(state_vector.shape), root.reshape(())


def relabel(tiles, names, order):
    count = len(names)
    places = [count - 1 - names.index(name) for name in order]
    picked = []
    for at in range(len(tiles)):
        bits = [(at >> (count - 1 - j)) & 1 for j in range(count)]
        picked.append(tiles[sum(bit << place for bit, place in zip(bits, places))])
    return picked


def lane_bit(size, lane):
    return lax.broadcasted_iota(jnp.int32, (8, size), 1) // lane % 2 == 1


def swap(tiles, names, major, lane):
    step = 1 << (len(names) - 1 - names.index(major))
    size = tiles[0].shape[1]
    second = lane_bit(size, lane)
    out = list(tiles)
    for at in range(len(tiles)):
        if not at & step:
            low, high = tiles[at], tiles[at + step]
            out[at] = jnp.where(second, pltpu.roll(high, lane, 1), low)
            out[at + step] = jnp.where(second, high, pltpu.roll(low, size - lane, 1))
    return out


def turn(tiles, names, majors, rolled=False, roll=True):
    count, size = len(majors), tiles[0].shape[1]
    many, group = 1 << count, size >> count
    steps = [1 << (len(names) - 1 - names.index(name)) for name in majors]
    places = [
        sum(step for j, step in enumerate(steps) if at >> (count - 1 - j) & 1)
        for at in range(many)
    ]
    picks = [lane_bit(size, group << j) for j in range(count)]
    out = list(tiles)
    for base in range(len(tiles)):
        if base & sum(steps):
            continue
        held = [tiles[base + place] for place in places]
        if not rolled:
            held = [held[0]] + [pltpu.roll(held[j], j * group, 1) for j in range(1, many)]
        held = [held[-j % many] for j in range(many)]
        for j, pick in enumerate(picks):
            held = [jnp.where(pick, held[(at - 2**j) % many], held[at]) for at in range(many)]
        for at, place in enumerate(places):
            turned = roll and at > 0
            out[base + place] = pltpu.roll(held[at], size - at * group, 1) if turned else held[at]
    return out


def wide_product(left, right):
    def one(a, b):
        return lax.dot_general(a, b, (((1,), (0,)), ((), ())), preferred_element_type=jnp.float32)

    count = right[0].shape[1]
    both = one(left[0], jnp.concatenate(right, axis=1))
    return both[:, :count] + (both[:, count:] + one(left[1], right[0]))


def split(values):
    return [values[at * 8 : (at + 1) * 8] for at in range(values.shape[0] // 8)]


def join(tiles):
    return jnp.concatenate(tiles, axis=0)


def rename(names, old, new):
    return [new if name == old else name for name in names]


def bits(name, count):
    return [name + str(j) for j in reversed(range(count))]


def fast_kernel(
    n_outer, n_inner, state_in, gates_in, early, last, scales,
    state, gates, sent_a, held_a, sent_b, landed, settled, part, sums, scaled, fetched,
    send_a, recv_a, send_b, recv_b, send_s, recv_s, own_s, moved,
):
    def fetch(at):
        if at == 0:
            return pltpu.make_async_copy(state_in, state, fetched.at[0])
        return pltpu.make_async_copy(gates_in.at[at - 1], gates.at[at - 1], fetched.at[at])

    dim = gates.shape[2]
    chunks = state.shape[1] // dim
    n_all = n_outer * n_inner
    o_bits, i_bits = n_outer.bit_length() - 1, n_inner.bit_length() - 1
    outer, inner = lax.axis_index("outer"), lax.axis_index("inner")
    me = outer * n_inner + inner

    plane = 2 * n_inner
    levels = n_all // plane
    span = levels // 2
    level, spot = me // plane, me % plane
    side = level // span

    def peer(k):
        j, p = k
        if j < span:
            to = (1 - side) * (levels - 1 - j) + side * j
        else:
            to = side * span + (level + j) % span
        to = to * plane + spot
        for q in range(i_bits + 1):
            if p >> q & 1:
                to = to + (1 - 2 * (spot // 2**q % 2)) * 2**q
        return to // n_inner, to % n_inner

    spots = sorted(range(plane), key=lambda p: (-p.bit_count(), -p))
    across = [(j, p) for j in range(span) for p in spots]
    beside = [(j, p) for j in reversed(range(span, levels)) for p in spots][:-1]
    order = [k for both in zip(across, beside) for k in both] + across[-1:]
    inward = sorted(beside, key=lambda k: k[0])
    opening = [k for both in zip(across, inward) for k in both] + across[-1:]
    barrier = pltpu.get_barrier_semaphore()
    for k in across + beside:
        pl.semaphore_signal(barrier, inc=1, device_id=peer(k), device_id_type=MESH)
    for at in (0, 1, 4, 2, 3):
        fetch(at).start()

    def remote(src, dst, send, recv, target):
        return pltpu.make_async_remote_copy(
            src_ref=src, dst_ref=dst, send_sem=send, recv_sem=recv,
            device_id=target, device_id_type=MESH,
        )

    def tile(ref, at):
        return ref.at[pl.ds(pl.multiple_of(at * 8, 8), 8), :]

    def trade(sent, held, send, recv, chunk, peers):
        for k in peers:
            a, b = peer(k)
            remote(
                tile(sent, a * n_inner + b), tile(held, me),
                send.at[chunk], recv.at[chunk], (a, b),
            ).start()

    def keep(sent, held, recv, chunk):
        pltpu.make_async_copy(
            tile(sent, me), tile(held, me), recv.at[chunk]
        ).start()

    def arrived(held, send, recv, chunk):
        remote(held, held, send.at[chunk], recv.at[chunk], (outer, inner)).wait_recv()

    def left(sent, send, recv, chunk):
        both = sent.at[pl.ds(0, (n_all - 1) * 8), :]
        remote(both, both, send.at[chunk], recv.at[chunk], (outer, inner)).wait_send()

    top = dim // 2
    fetch(1).wait()

    def rows0(c):
        return jnp.concatenate(
            [
                gates[0, c, pl.ds(high * top + low, top // 2, stride=2), :]
                for high in range(2)
                for low in range(2)
            ],
            axis=0,
        )

    first = complex_matrix(rows0(0), rows0(1))
    fetch(4).wait()
    real, imag = gates[3, 0], gates[3, 1]
    low = []
    for high in range(2):
        rows = slice(high * top, (high + 1) * top)
        low.append(jnp.concatenate([real[rows], -imag[rows]], axis=1))
        low.append(jnp.concatenate([imag[rows], real[rows]], axis=1))
    low = halves(jnp.concatenate(low, axis=0))
    fetch(0).wait()
    for chunk in range(chunks):
        values = jnp.concatenate(
            [state[c, chunk * dim : (chunk + 1) * dim, :] for c in range(2)], axis=0
        )
        values = product(first, halves(values), ((1,), (0,)))
        wide = jnp.concatenate([values[:dim], values[dim:]], axis=1)
        wide = product(halves(wide), low, ((1,), (1,)))
        tiles = split(jnp.concatenate([wide[:, :dim], wide[:, dim:]], axis=0))
        names = ["b6", "b13", "b7", "b12", "b11"]
        tiles = swap(tiles, names, "b11", dim // 4)
        names = rename(names, "b11", "b5")
        tiles = swap(tiles, names, "b12", dim // 8)
        names = rename(names, "b12", "b4")
        tiles = relabel(tiles, names, ["b6", "b13", "b7", "b5", "b4"])
        sent_a[chunk] = pltpu.roll(join(tiles), inner * (dim // n_inner), 1)
        keep(sent_a.at[chunk], held_a.at[chunk], recv_a, chunk)
        if chunk > 0:
            trade(sent_a.at[chunk], held_a.at[chunk], send_a, recv_a, chunk, order)
            continue
        pl.semaphore_wait(barrier, n_all - 1)
        trade(sent_a.at[chunk], held_a.at[chunk], send_a, recv_a, chunk, opening)

    fetch(2).wait()
    second = complex_matrix(gates[1, 0], gates[1, 1])
    fetch(3).wait()
    third = complex_matrix(gates[2, 0], gates[2, 1])
    o_names, i_names = bits("o", o_bits), bits("i", i_bits)
    home = [landed.at[chunk] for chunk in range(chunks - 1)] + [last]
    total = jnp.zeros((1, dim), jnp.float32)
    for chunk in range(chunks):
        arrived(held_a.at[chunk], send_a, recv_a, chunk)
        tiles = turn(split(held_a[chunk]), o_names + i_names, i_names, rolled=True)
        names = o_names + ["c", "b11"]
        rows = ["c"] + o_names + ["b11"]
        values = wide_product(second, halves(join(relabel(tiles, names, rows))))
        tiles = turn(split(values), rows, o_names)
        names = ["c"] + i_names + ["b12", "b11"]
        rows = ["c"] + i_names + ["b12", "b11"]
        values = wide_product(third, halves(join(relabel(tiles, names, rows))))
        total = total + jnp.sum(values * values, axis=0, keepdims=True)
        if chunk == chunks - 1:
            part[...] = total
            for k in order:
                remote(part, sums.at[me], send_s, recv_s, peer(k)).start()
            pltpu.make_async_copy(part, sums.at[me], own_s).start()
        tiles = turn(split(values), rows, ["c", "b11", "b12"], roll=False)
        names = ["o2"] + i_names + ["o0", "o1"]
        sent_b[chunk] = join(relabel(tiles, names, o_names + i_names))
        peers = order if chunk == chunks - 1 else across + beside
        trade(sent_b.at[chunk], home[chunk], send_b, recv_b, chunk, peers)
        keep(sent_b.at[chunk], home[chunk], recv_b, chunk)

    moves = []
    for chunk in range(chunks - 1):
        arrived(home[chunk], send_b, recv_b, chunk)
        settle(landed[chunk], outer, settled.at[chunk], None)
        moves.append(pltpu.make_async_copy(settled.at[chunk], early.at[chunk], moved.at[chunk]))
        moves[-1].start()
    everyone = sums.at[pl.ds(0, n_all - 1)]
    remote(everyone, everyone, send_s, recv_s, (outer, inner)).wait()
    pltpu.make_async_copy(part, sums.at[me], own_s).wait()
    whole = jnp.sum(jnp.sum(sums[...], axis=0), axis=1, keepdims=True)
    root = jnp.sqrt(whole / (n_all * chunks * dim * dim))
    scaled[:8, :] = jnp.broadcast_to(1.0 / root, (8, dim))
    scaled[8:, :] = jnp.broadcast_to(root, (8, dim))
    moves.append(pltpu.make_async_copy(scaled, scales, moved.at[chunks - 1]))
    moves[-1].start()
    for chunk in range(chunks):
        left(sent_a.at[chunk], send_a, recv_a, chunk)
    for move in moves:
        move.wait()
    for chunk in range(chunks):
        left(sent_b.at[chunk], send_b, recv_b, chunk)
    arrived(last, send_b, recv_b, chunks - 1)


def settle(values, outer, out, scale):
    size = values.shape[1]
    ahead = [(size + (j - outer) * (size // 8)) % size for j in range(8)]
    tiles = split(values)
    for at in range(len(tiles)):
        tiles[at] = pltpu.roll(tiles[at], ahead[4 * (at >> 4) + (at & 3)], 1)
    names = ["b6", "b13", "b7", "b5", "b4"]
    tiles = turn(tiles, names, ["b6", "b5", "b4"], rolled=True)
    names = ["c", "b13", "b7", "b11", "b12"]
    tiles = relabel(tiles, names, ["c", "b13", "b12", "b11", "b7"])
    for at in range(len(tiles)):
        c, rest = divmod(at, len(tiles) // 2)
        kept = tiles[at] if scale is None else tiles[at] * scale
        out[c, pl.ds(rest // 2 * 16 + rest % 2, 8, stride=2), :] = kept


def fast_finish(early, last, scales, out, rms):
    count, _, half, dim = early.shape
    scale = scales[:8, :]
    rms[...] = scales[8:9, :1]
    for chunk in range(count):
        for c in range(2):
            values = early[chunk, c].reshape(-1, 8, dim) * scale[None]
            out[c, chunk * half : (chunk + 1) * half, :] = values.reshape(half, dim)
    outer = lax.axis_index("outer")
    settle(last[...], outer, out.at[:, pl.ds(count * half, half), :], scale)


def fast_shards(n_outer, n_inner, state_vector, gate_matrices):
    dim = gate_matrices.shape[2]
    rows = state_vector.shape[3] // dim
    chunks = rows // dim
    n_all = n_outer * n_inner
    held = pltpu.VMEM((chunks, n_all * 8, dim), jnp.float32)
    dma = pltpu.SemaphoreType.DMA
    vmem = pl.BlockSpec(memory_space=pltpu.VMEM)
    hbm = pl.BlockSpec(memory_space=pltpu.HBM)
    anywhere = pl.BlockSpec(memory_space=pl.ANY)
    early = (chunks - 1, 2, dim, dim)
    held_values = pl.pallas_call(
        functools.partial(fast_kernel, n_outer, n_inner),
        out_shape=(
            jax.ShapeDtypeStruct(early, jnp.float32),
            jax.ShapeDtypeStruct((n_all * 8, dim), jnp.float32),
            jax.ShapeDtypeStruct((16, dim), jnp.float32),
        ),
        in_specs=[hbm, hbm],
        out_specs=(anywhere, anywhere, anywhere),
        scratch_shapes=[
            pltpu.VMEM((2, rows, dim), jnp.float32),
            pltpu.VMEM(gate_matrices.shape, jnp.float32),
        ]
        + [held] * 3
        + [pltpu.VMEM((chunks - 1, n_all * 8, dim), jnp.float32), pltpu.VMEM(early, jnp.float32)]
        + [pltpu.VMEM(shape, jnp.float32) for shape in ((1, dim), (n_all, 1, dim), (16, dim))]
        + [dma((5,))]
        + [dma((chunks,))] * 4
        + [dma(())] * 3
        + [dma((chunks,))],
        compiler_params=pltpu.CompilerParams(
            collective_id=0, has_side_effects=True, vmem_limit_bytes=TRADE_LIMIT
        ),
    )(state_vector.reshape(2, rows, dim), gate_matrices)
    final_state, root = pl.pallas_call(
        fast_finish,
        out_shape=(
            jax.ShapeDtypeStruct((2, rows, dim), jnp.float32),
            jax.ShapeDtypeStruct((1, 1), jnp.float32),
        ),
        in_specs=[vmem, vmem, vmem],
        out_specs=(vmem, vmem),
        compiler_params=pltpu.CompilerParams(vmem_limit_bytes=LIMIT),
    )(*held_values)
    return final_state.reshape(state_vector.shape), root.reshape(())


def fits(n_outer, n_inner, state_vector, gate_matrices):
    dim = gate_matrices.shape[2]
    rows = state_vector.shape[3] // dim
    return (
        rows == 2 * dim
        and n_outer * n_inner * 8 == 2 * dim
        and dim == n_outer * 16
        and dim == n_inner * 32
    )


def shards_of(n_outer, n_inner, state_vector, gate_matrices):
    run = fast_shards if fits(n_outer, n_inner, state_vector, gate_matrices) else shards
    return run(n_outer, n_inner, state_vector, gate_matrices)


def solution(mesh):
    in_specs = (P(None, "outer", "inner", None), P())
    out_specs = (P(None, "outer", "inner", None), P())
    body = functools.partial(shards_of, mesh.shape["outer"], mesh.shape["inner"])
    return jax.shard_map(body, mesh=mesh, in_specs=in_specs, out_specs=out_specs, check_vma=False)
```

```python
import functools

import jax
import jax.numpy as jnp
from jax import lax
from jax.experimental import pallas as pl
from jax.experimental.pallas import tpu as pltpu
from jax.sharding import PartitionSpec as P

MESH = pl.DeviceIdType.MESH
TRADE_LIMIT = 56_150_000
LIMIT = 16 * 1024 * 1024


def halves(values):
    high = values.astype(jnp.bfloat16)
    low = (values - high.astype(jnp.float32)).astype(jnp.bfloat16)
    return high, low


def product(left, right, dims):
    def one(a, b):
        return lax.dot_general(a, b, (dims, ((), ())), preferred_element_type=jnp.float32)

    return one(left[0], right[0]) + (one(left[0], right[1]) + one(left[1], right[0]))


def complex_matrix(real, imag):
    top = jnp.concatenate([real, -imag], axis=1)
    bottom = jnp.concatenate([imag, real], axis=1)
    return halves(jnp.concatenate([top, bottom], axis=0))


def spread(position, count):
    half, rest = count // 2, position // 2
    return (position % 2) * half + (rest % 2) * (half // 2) + rest // 2


def kernel(
    n_outer, n_inner, chunks, state_in, gates_in, held_c, sums,
    state, gates, sent_a, held_a, sent_b, held_b, sent_c, part, fetched,
    send_a, recv_a, send_b, recv_b, send_c, recv_c, send_s, recv_s,
):
    def fetch(at):
        if at == 0:
            return pltpu.make_async_copy(state_in, state, fetched.at[0])
        return pltpu.make_async_copy(gates_in.at[at - 1], gates.at[at - 1], fetched.at[at])

    for at in (0, 1, 4, 2, 3):
        fetch(at).start()
    dim = gates.shape[2]
    passive = state.shape[1] // dim
    sub = passive // chunks
    step = dim // chunks
    rows_outer = dim // n_outer * sub
    rows_inner = dim // n_inner * sub
    ratio = n_outer // n_inner
    n_all = n_outer * n_inner
    outer, inner = lax.axis_index("outer"), lax.axis_index("inner")
    me = outer * n_inner + inner

    def block(ref, chunk, at, rows):
        return ref.at[chunk, :, pl.ds(pl.multiple_of(at * rows, rows), rows), :]

    def remote(src, dst, send, recv, target):
        return pltpu.make_async_remote_copy(
            src_ref=src, dst_ref=dst, send_sem=send, recv_sem=recv,
            device_id=target, device_id_type=MESH,
        )

    far_first = sorted(range(n_outer), key=lambda k: abs(2 * k - n_outer))

    def everyone(act):
        if n_all > 64:

            def body(k, carry):
                one(act, k // n_inner, k % n_inner)
                return carry

            lax.fori_loop(1, n_all, body, 0)
            return
        for a in far_first:
            for b in range(n_inner):
                if a or b:
                    one(act, a, b)

    def one(act, a, b):
        ahead = ((outer + a) % n_outer, (inner + b) % n_inner)
        behind = ((outer + n_outer - a) % n_outer, (inner + n_inner - b) % n_inner)
        act(a * n_inner + b, ahead, behind)

    barrier = pltpu.get_barrier_semaphore()

    for k in range(1, n_outer):
        pl.semaphore_signal(
            barrier, inc=1, device_id=((outer + k) % n_outer, inner), device_id_type=MESH
        )
    for k in range(1, n_inner):
        pl.semaphore_signal(
            barrier, inc=1, device_id=(outer, (inner + k) % n_inner), device_id_type=MESH
        )

    def load(ref, chunk):
        return jnp.concatenate(
            [
                jnp.concatenate(
                    [ref[chunk, c, pl.ds(b, dim, stride=sub), :] for b in range(sub)], axis=1
                )
                for c in range(2)
            ],
            axis=0,
        )

    def store(ref, chunk, values):
        for c in range(2):
            for b in range(sub):
                ref[chunk, c, pl.ds(b, dim, stride=sub), :] = values[
                    c * dim : (c + 1) * dim, b * dim : (b + 1) * dim
                ]

    def low_gate(values):
        rows = values.shape[0] // 2
        matrix = complex_matrix(gates[3, 0], gates[3, 1])
        columns = []
        for b in range(values.shape[1] // dim):
            both = values[:, b * dim : (b + 1) * dim]
            wide = jnp.concatenate([both[:rows], both[rows:]], axis=1)
            wide = product(halves(wide), matrix, ((1,), (1,)))
            columns.append(jnp.concatenate([wide[:, :dim], wide[:, dim:]], axis=0))
        return jnp.concatenate(columns, axis=1)

    fetch(0).wait()
    fetch(1).wait()
    first = halves(
        jnp.concatenate(
            [
                jnp.concatenate(
                    [state[c, w * dim : (w + 1) * dim, :] for w in range(passive)], axis=1
                )
                for c in range(2)
            ],
            axis=0,
        )
    )

    def trade_a(chunk):
        for k in far_first[:-1]:
            to = (outer + k) % n_outer
            remote(
                block(sent_a, chunk, spread(to, n_outer), rows_outer),
                block(held_a, chunk, outer, rows_outer),
                send_a.at[chunk, to], recv_a.at[chunk, outer], (to, inner),
            ).start()
        pltpu.make_async_copy(
            block(sent_a, chunk, spread(outer, n_outer), rows_outer),
            block(held_a, chunk, outer, rows_outer),
            recv_a.at[chunk, outer],
        ).start()

    for chunk in range(chunks):
        pick = pl.ds(chunk, step, stride=chunks)
        matrix = complex_matrix(gates[0, 0, pick, :], gates[0, 1, pick, :])
        values = product(matrix, first, ((1,), (0,)))
        if chunk > 0:
            if chunk == 1:
                fetch(4).wait()
            values = low_gate(values)
        for c in range(2):
            for w in range(passive):
                sent_a[chunk, c, w * step : (w + 1) * step, :] = values[
                    c * step : (c + 1) * step, w * dim : (w + 1) * dim
                ]
        if chunk == 0:
            pl.semaphore_wait(barrier, n_outer + n_inner - 2)
        trade_a(chunk)

    fetch(2).wait()
    matrix = complex_matrix(gates[1, 0], gates[1, 1])
    mine = spread(outer, n_outer)
    column, within = mine // ratio, mine % ratio
    slot = inner * ratio + within
    for chunk in range(chunks):
        for k in range(n_outer):
            spot = block(held_a, chunk, k, rows_outer)
            remote(spot, spot, send_a.at[chunk, k], recv_a.at[chunk, k], (outer, inner)).wait_recv()
        values = halves(load(held_a, chunk))
        store(sent_b, chunk, product(matrix, values, ((1,), (0,))))
        for k in far_first:
            to = (outer + k) % n_outer
            src = block(sent_b, chunk, to, rows_outer)
            dst = block(held_b, chunk, slot, rows_outer)
            copy = remote(
                src, dst, send_b.at[chunk, to], recv_b.at[chunk, slot], (to, column)
            )
            if k > 0:
                copy.start()
            else:
                pl.when(column != inner)(copy.start)
                pl.when(column == inner)(
                    pltpu.make_async_copy(src, dst, recv_b.at[chunk, slot]).start
                )

    fetch(3).wait()
    matrix = complex_matrix(gates[2, 0], gates[2, 1])
    total = jnp.zeros((1, dim), jnp.float32)
    own = pltpu.make_async_copy(part, sums.at[me], recv_s.at[0])

    def share(k, ahead, behind):
        remote(part, sums.at[me], send_s.at[k], recv_s.at[k], ahead).start()

    for chunk in range(chunks):
        for k in range(n_outer):
            spot = block(held_b, chunk, k, rows_outer)
            remote(spot, spot, send_b.at[chunk, k], recv_b.at[chunk, k], (outer, inner)).wait_recv()
        values = product(matrix, halves(load(held_b, chunk)), ((1,), (0,)))
        if chunk == 0:
            if chunks == 1:
                fetch(4).wait()
            values = low_gate(values)
        for b in range(sub):
            piece = values[:, b * dim : (b + 1) * dim]
            total = total + jnp.sum(piece * piece, axis=0, keepdims=True)
        if chunk == chunks - 1:
            part[...] = total
            everyone(share)
            own.start()
        store(sent_c, chunk, values)
        for k in range(1, n_inner):
            to = (inner + k) % n_inner
            remote(
                block(sent_c, chunk, to, rows_inner),
                block(held_c, chunk, inner, rows_inner),
                send_c.at[chunk, to], recv_c.at[chunk, inner], (outer, to),
            ).start()
        pltpu.make_async_copy(
            block(sent_c, chunk, inner, rows_inner),
            block(held_c, chunk, inner, rows_inner),
            recv_c.at[chunk, inner],
        ).start()

    def arrived(k, ahead, behind):
        spot = sums.at[behind[0] * n_inner + behind[1]]
        remote(part, spot, send_s.at[k], recv_s.at[k], ahead).wait_recv()

    def left(k, ahead, behind):
        remote(part, sums.at[me], send_s.at[k], recv_s.at[k], ahead).wait_send()

    for chunk in range(chunks):
        for k in range(n_inner):
            spot = block(held_c, chunk, k, rows_inner)
            remote(spot, spot, send_c.at[chunk, k], recv_c.at[chunk, k], (outer, inner)).wait_recv()

    for chunk in range(chunks):
        for k in range(1, n_outer):
            to = (outer + k) % n_outer
            spot = block(sent_a, chunk, to, rows_outer)
            remote(spot, spot, send_a.at[chunk, to], recv_a.at[chunk, to], (to, inner)).wait_send()
        for k in range(n_outer):
            to = (outer + k) % n_outer
            spot = block(sent_b, chunk, to, rows_outer)
            copy = remote(spot, spot, send_b.at[chunk, to], recv_b.at[chunk, to], (to, column))
            if k > 0:
                copy.wait_send()
            else:
                pl.when(column != inner)(copy.wait_send)
        for k in range(1, n_inner):
            to = (inner + k) % n_inner
            spot = block(sent_c, chunk, to, rows_inner)
            remote(spot, spot, send_c.at[chunk, to], recv_c.at[chunk, to], (outer, to)).wait_send()
    everyone(left)
    own.wait()
    everyone(arrived)


def finish(n_all, values, sums, out, rms):
    chunks, _, rows, dim = values.shape
    whole = jnp.sum(jnp.sum(sums[...], axis=0), axis=1, keepdims=True)
    root = jnp.sqrt(whole / (n_all * chunks * rows * dim))
    rms[...] = root
    scale = jnp.broadcast_to(1.0 / root, (8, dim))
    for chunk in range(chunks):
        for c in range(2):
            scaled = values[chunk, c].reshape(-1, 8, dim) * scale[None]
            out[c, pl.ds(chunk, rows, stride=chunks), :] = scaled.reshape(-1, dim)


def shards(n_outer, n_inner, state_vector, gate_matrices):
    dim = gate_matrices.shape[2]
    amp_count = state_vector.shape[3]
    rows = amp_count // dim
    passive = rows // dim
    chunks = passive if (dim // n_outer) % 8 == 0 else 1
    held = pltpu.VMEM((chunks, 2, rows // chunks, dim), jnp.float32)
    n_all = n_outer * n_inner
    dma = pltpu.SemaphoreType.DMA
    vmem = pl.BlockSpec(memory_space=pltpu.VMEM)
    hbm = pl.BlockSpec(memory_space=pltpu.HBM)
    anywhere = pl.BlockSpec(memory_space=pl.ANY)
    values, sums = pl.pallas_call(
        functools.partial(kernel, n_outer, n_inner, chunks),
        out_shape=(
            jax.ShapeDtypeStruct((chunks, 2, rows // chunks, dim), jnp.float32),
            jax.ShapeDtypeStruct((n_all, 1, dim), jnp.float32),
        ),
        in_specs=[hbm, hbm],
        out_specs=(anywhere, anywhere),
        scratch_shapes=[
            pltpu.VMEM((2, rows, dim), jnp.float32),
            pltpu.VMEM(gate_matrices.shape, jnp.float32),
        ]
        + [held] * 5
        + [pltpu.VMEM((1, dim), jnp.float32), dma((5,))]
        + [dma((chunks, n_outer))] * 4
        + [dma((chunks, n_inner))] * 2
        + [dma((n_all,))] * 2,
        compiler_params=pltpu.CompilerParams(
            collective_id=0, has_side_effects=True, vmem_limit_bytes=TRADE_LIMIT
        ),
    )(state_vector.reshape(2, rows, dim), gate_matrices)
    final_state, root = pl.pallas_call(
        functools.partial(finish, n_all),
        out_shape=(
            jax.ShapeDtypeStruct((2, rows, dim), jnp.float32),
            jax.ShapeDtypeStruct((1, 1), jnp.float32),
        ),
        in_specs=[vmem, vmem],
        out_specs=(vmem, vmem),
        compiler_params=pltpu.CompilerParams(vmem_limit_bytes=LIMIT),
    )(values, sums)
    return final_state.reshape(state_vector.shape), root.reshape(())


def relabel(tiles, names, order):
    count = len(names)
    places = [count - 1 - names.index(name) for name in order]
    picked = []
    for at in range(len(tiles)):
        bits = [(at >> (count - 1 - j)) & 1 for j in range(count)]
        picked.append(tiles[sum(bit << place for bit, place in zip(bits, places))])
    return picked


def lane_bit(size, lane):
    return lax.broadcasted_iota(jnp.int32, (8, size), 1) // lane % 2 == 1


def swap(tiles, names, major, lane):
    step = 1 << (len(names) - 1 - names.index(major))
    size = tiles[0].shape[1]
    second = lane_bit(size, lane)
    out = list(tiles)
    for at in range(len(tiles)):
        if not at & step:
            low, high = tiles[at], tiles[at + step]
            out[at] = jnp.where(second, pltpu.roll(high, lane, 1), low)
            out[at + step] = jnp.where(second, high, pltpu.roll(low, size - lane, 1))
    return out


def turn(tiles, names, majors, rolled=False, roll=True):
    count, size = len(majors), tiles[0].shape[1]
    many, group = 1 << count, size >> count
    steps = [1 << (len(names) - 1 - names.index(name)) for name in majors]
    places = [
        sum(step for j, step in enumerate(steps) if at >> (count - 1 - j) & 1)
        for at in range(many)
    ]
    picks = [lane_bit(size, group << j) for j in range(count)]
    out = list(tiles)
    for base in range(len(tiles)):
        if base & sum(steps):
            continue
        held = [tiles[base + place] for place in places]
        if not rolled:
            held = [held[0]] + [pltpu.roll(held[j], j * group, 1) for j in range(1, many)]
        held = [held[-j % many] for j in range(many)]
        for j, pick in enumerate(picks):
            held = [jnp.where(pick, held[(at - 2**j) % many], held[at]) for at in range(many)]
        for at, place in enumerate(places):
            turned = roll and at > 0
            out[base + place] = pltpu.roll(held[at], size - at * group, 1) if turned else held[at]
    return out


def wide_product(left, right):
    def one(a, b):
        return lax.dot_general(a, b, (((1,), (0,)), ((), ())), preferred_element_type=jnp.float32)

    count = right[0].shape[1]
    both = one(left[0], jnp.concatenate(right, axis=1))
    return both[:, :count] + (both[:, count:] + one(left[1], right[0]))


def split(values):
    return [values[at * 8 : (at + 1) * 8] for at in range(values.shape[0] // 8)]


def join(tiles):
    return jnp.concatenate(tiles, axis=0)


def rename(names, old, new):
    return [new if name == old else name for name in names]


def bits(name, count):
    return [name + str(j) for j in reversed(range(count))]


def fast_kernel(
    n_outer, n_inner, state_in, gates_in, early, last, scales,
    state, gates, sent_a, held_a, sent_b, landed, settled, part, sums, scaled, fetched,
    send_a, recv_a, send_b, recv_b, send_s, recv_s, own_s, moved,
):
    def fetch(at):
        if at == 0:
            return pltpu.make_async_copy(state_in, state, fetched.at[0])
        return pltpu.make_async_copy(gates_in.at[at - 1], gates.at[at - 1], fetched.at[at])

    dim = gates.shape[2]
    chunks = state.shape[1] // dim
    n_all = n_outer * n_inner
    o_bits, i_bits = n_outer.bit_length() - 1, n_inner.bit_length() - 1
    outer, inner = lax.axis_index("outer"), lax.axis_index("inner")
    me = outer * n_inner + inner

    plane = 2 * n_inner
    levels = n_all // plane
    span = levels // 2
    level, spot = me // plane, me % plane
    side = level // span

    def peer(k):
        j, p = k
        if j < span:
            to = (1 - side) * (levels - 1 - j) + side * j
        else:
            to = side * span + (level + j) % span
        to = to * plane + spot
        for q in range(i_bits + 1):
            if p >> q & 1:
                to = to + (1 - 2 * (spot // 2**q % 2)) * 2**q
        return to // n_inner, to % n_inner

    spots = sorted(range(plane), key=lambda p: (-p.bit_count(), -p))
    across = [(j, p) for j in range(span) for p in spots]
    beside = [(j, p) for j in reversed(range(span, levels)) for p in spots][:-1]
    order = [k for both in zip(across, beside) for k in both] + across[-1:]
    inward = sorted(beside, key=lambda k: k[0])
    opening = [k for both in zip(across, inward) for k in both] + across[-1:]
    barrier = pltpu.get_barrier_semaphore()
    for k in across + beside:
        pl.semaphore_signal(barrier, inc=1, device_id=peer(k), device_id_type=MESH)
    for at in (0, 1, 4, 2, 3):
        fetch(at).start()

    def remote(src, dst, send, recv, target):
        return pltpu.make_async_remote_copy(
            src_ref=src, dst_ref=dst, send_sem=send, recv_sem=recv,
            device_id=target, device_id_type=MESH,
        )

    def tile(ref, at):
        return ref.at[pl.ds(pl.multiple_of(at * 8, 8), 8), :]

    def trade(sent, held, send, recv, chunk, peers):
        for k in peers:
            a, b = peer(k)
            remote(
                tile(sent, a * n_inner + b), tile(held, me),
                send.at[chunk], recv.at[chunk], (a, b),
            ).start()

    def keep(sent, held, recv, chunk):
        pltpu.make_async_copy(
            tile(sent, me), tile(held, me), recv.at[chunk]
        ).start()

    def arrived(held, send, recv, chunk):
        remote(held, held, send.at[chunk], recv.at[chunk], (outer, inner)).wait_recv()

    def left(sent, send, recv, chunk):
        both = sent.at[pl.ds(0, (n_all - 1) * 8), :]
        remote(both, both, send.at[chunk], recv.at[chunk], (outer, inner)).wait_send()

    top = dim // 2
    fetch(1).wait()

    def rows0(c):
        return jnp.concatenate(
            [
                gates[0, c, pl.ds(high * top + low, top // 2, stride=2), :]
                for high in range(2)
                for low in range(2)
            ],
            axis=0,
        )

    first = complex_matrix(rows0(0), rows0(1))
    fetch(4).wait()
    real, imag = gates[3, 0], gates[3, 1]
    low = []
    for high in range(2):
        rows = slice(high * top, (high + 1) * top)
        low.append(jnp.concatenate([real[rows], -imag[rows]], axis=1))
        low.append(jnp.concatenate([imag[rows], real[rows]], axis=1))
    low = halves(jnp.concatenate(low, axis=0))
    fetch(0).wait()
    for chunk in range(chunks):
        values = jnp.concatenate(
            [state[c, chunk * dim : (chunk + 1) * dim, :] for c in range(2)], axis=0
        )
        values = product(first, halves(values), ((1,), (0,)))
        wide = jnp.concatenate([values[:dim], values[dim:]], axis=1)
        wide = product(halves(wide), low, ((1,), (1,)))
        tiles = split(jnp.concatenate([wide[:, :dim], wide[:, dim:]], axis=0))
        names = ["b6", "b13", "b7", "b12", "b11"]
        tiles = swap(tiles, names, "b11", dim // 4)
        names = rename(names, "b11", "b5")
        tiles = swap(tiles, names, "b12", dim // 8)
        names = rename(names, "b12", "b4")
        tiles = relabel(tiles, names, ["b6", "b13", "b7", "b5", "b4"])
        sent_a[chunk] = pltpu.roll(join(tiles), inner * (dim // n_inner), 1)
        keep(sent_a.at[chunk], held_a.at[chunk], recv_a, chunk)
        if chunk > 0:
            trade(sent_a.at[chunk], held_a.at[chunk], send_a, recv_a, chunk, order)
            continue
        pl.semaphore_wait(barrier, n_all - 1)
        trade(sent_a.at[chunk], held_a.at[chunk], send_a, recv_a, chunk, opening)

    fetch(2).wait()
    second = complex_matrix(gates[1, 0], gates[1, 1])
    fetch(3).wait()
    third = complex_matrix(gates[2, 0], gates[2, 1])
    o_names, i_names = bits("o", o_bits), bits("i", i_bits)
    home = [landed.at[chunk] for chunk in range(chunks - 1)] + [last]
    total = jnp.zeros((1, dim), jnp.float32)
    for chunk in range(chunks):
        arrived(held_a.at[chunk], send_a, recv_a, chunk)
        tiles = turn(split(held_a[chunk]), o_names + i_names, i_names, rolled=True)
        names = o_names + ["c", "b11"]
        rows = ["c"] + o_names + ["b11"]
        values = wide_product(second, halves(join(relabel(tiles, names, rows))))
        tiles = turn(split(values), rows, o_names)
        names = ["c"] + i_names + ["b12", "b11"]
        rows = ["c"] + i_names + ["b12", "b11"]
        values = wide_product(third, halves(join(relabel(tiles, names, rows))))
        total = total + jnp.sum(values * values, axis=0, keepdims=True)
        if chunk == chunks - 1:
            part[...] = total
            for k in order:
                remote(part, sums.at[me], send_s, recv_s, peer(k)).start()
            pltpu.make_async_copy(part, sums.at[me], own_s).start()
        tiles = turn(split(values), rows, ["c", "b11", "b12"], roll=False)
        names = ["o2"] + i_names + ["o0", "o1"]
        sent_b[chunk] = join(relabel(tiles, names, o_names + i_names))
        peers = order if chunk == chunks - 1 else across + beside
        keep(sent_b.at[chunk], home[chunk], recv_b, chunk)
        trade(sent_b.at[chunk], home[chunk], send_b, recv_b, chunk, peers)

    moves = []
    for chunk in range(chunks - 1):
        arrived(home[chunk], send_b, recv_b, chunk)
        settle(landed[chunk], outer, settled.at[chunk], None)
        moves.append(pltpu.make_async_copy(settled.at[chunk], early.at[chunk], moved.at[chunk]))
        moves[-1].start()
    everyone = sums.at[pl.ds(0, n_all - 1)]
    remote(everyone, everyone, send_s, recv_s, (outer, inner)).wait()
    pltpu.make_async_copy(part, sums.at[me], own_s).wait()
    whole = jnp.sum(jnp.sum(sums[...], axis=0), axis=1, keepdims=True)
    root = jnp.sqrt(whole / (n_all * chunks * dim * dim))
    scaled[:8, :] = jnp.broadcast_to(1.0 / root, (8, dim))
    scaled[8:, :] = jnp.broadcast_to(root, (8, dim))
    moves.append(pltpu.make_async_copy(scaled, scales, moved.at[chunks - 1]))
    moves[-1].start()
    for chunk in range(chunks):
        left(sent_a.at[chunk], send_a, recv_a, chunk)
    for move in moves:
        move.wait()
    for chunk in range(chunks):
        left(sent_b.at[chunk], send_b, recv_b, chunk)
    arrived(last, send_b, recv_b, chunks - 1)


def settle(values, outer, out, scale):
    size = values.shape[1]
    ahead = [(size + (j - outer) * (size // 8)) % size for j in range(8)]
    tiles = split(values)
    for at in range(len(tiles)):
        tiles[at] = pltpu.roll(tiles[at], ahead[4 * (at >> 4) + (at & 3)], 1)
    names = ["b6", "b13", "b7", "b5", "b4"]
    tiles = turn(tiles, names, ["b6", "b5", "b4"], rolled=True)
    names = ["c", "b13", "b7", "b11", "b12"]
    tiles = relabel(tiles, names, ["c", "b13", "b12", "b11", "b7"])
    for at in range(len(tiles)):
        c, rest = divmod(at, len(tiles) // 2)
        kept = tiles[at] if scale is None else tiles[at] * scale
        out[c, pl.ds(rest // 2 * 16 + rest % 2, 8, stride=2), :] = kept


def fast_finish(early, last, scales, out, rms):
    count, _, half, dim = early.shape
    scale = scales[:8, :]
    rms[...] = scales[8:9, :1]
    for chunk in range(count):
        for c in range(2):
            values = early[chunk, c].reshape(-1, 8, dim) * scale[None]
            out[c, chunk * half : (chunk + 1) * half, :] = values.reshape(half, dim)
    outer = lax.axis_index("outer")
    settle(last[...], outer, out.at[:, pl.ds(count * half, half), :], scale)


def fast_shards(n_outer, n_inner, state_vector, gate_matrices):
    dim = gate_matrices.shape[2]
    rows = state_vector.shape[3] // dim
    chunks = rows // dim
    n_all = n_outer * n_inner
    held = pltpu.VMEM((chunks, n_all * 8, dim), jnp.float32)
    dma = pltpu.SemaphoreType.DMA
    vmem = pl.BlockSpec(memory_space=pltpu.VMEM)
    hbm = pl.BlockSpec(memory_space=pltpu.HBM)
    anywhere = pl.BlockSpec(memory_space=pl.ANY)
    early = (chunks - 1, 2, dim, dim)
    held_values = pl.pallas_call(
        functools.partial(fast_kernel, n_outer, n_inner),
        out_shape=(
            jax.ShapeDtypeStruct(early, jnp.float32),
            jax.ShapeDtypeStruct((n_all * 8, dim), jnp.float32),
            jax.ShapeDtypeStruct((16, dim), jnp.float32),
        ),
        in_specs=[hbm, hbm],
        out_specs=(anywhere, anywhere, anywhere),
        scratch_shapes=[
            pltpu.VMEM((2, rows, dim), jnp.float32),
            pltpu.VMEM(gate_matrices.shape, jnp.float32),
        ]
        + [held] * 3
        + [pltpu.VMEM((chunks - 1, n_all * 8, dim), jnp.float32), pltpu.VMEM(early, jnp.float32)]
        + [pltpu.VMEM(shape, jnp.float32) for shape in ((1, dim), (n_all, 1, dim), (16, dim))]
        + [dma((5,))]
        + [dma((chunks,))] * 4
        + [dma(())] * 3
        + [dma((chunks,))],
        compiler_params=pltpu.CompilerParams(
            collective_id=0, has_side_effects=True, vmem_limit_bytes=TRADE_LIMIT
        ),
    )(state_vector.reshape(2, rows, dim), gate_matrices)
    final_state, root = pl.pallas_call(
        fast_finish,
        out_shape=(
            jax.ShapeDtypeStruct((2, rows, dim), jnp.float32),
            jax.ShapeDtypeStruct((1, 1), jnp.float32),
        ),
        in_specs=[vmem, vmem, vmem],
        out_specs=(vmem, vmem),
        compiler_params=pltpu.CompilerParams(vmem_limit_bytes=LIMIT),
    )(*held_values)
    return final_state.reshape(state_vector.shape), root.reshape(())


def fits(n_outer, n_inner, state_vector, gate_matrices):
    dim = gate_matrices.shape[2]
    rows = state_vector.shape[3] // dim
    return (
        rows == 2 * dim
        and n_outer * n_inner * 8 == 2 * dim
        and dim == n_outer * 16
        and dim == n_inner * 32
    )


def shards_of(n_outer, n_inner, state_vector, gate_matrices):
    run = fast_shards if fits(n_outer, n_inner, state_vector, gate_matrices) else shards
    return run(n_outer, n_inner, state_vector, gate_matrices)


def solution(mesh):
    in_specs = (P(None, "outer", "inner", None), P())
    out_specs = (P(None, "outer", "inner", None), P())
    body = functools.partial(shards_of, mesh.shape["outer"], mesh.shape["inner"])
    return jax.shard_map(body, mesh=mesh, in_specs=in_specs, out_specs=out_specs, check_vma=False)
```
